32 devices in a mesh: chan: 8 (over y, x, core), sub: 4 (over z).
Axes of the slice: x: 2, y: 2, z: 4, core: 2. Of those that a mesh axis runs over, the one named last changes fastest.
Arguments:
- spectra: bfloat16 [4, 2, 512, 32768], P('sub', None, None, 'chan'), may hold values from -12 to 12
- filter_init: float32 [2, 32768], P(None, 'chan'), may hold values from -2.1 to 2.1
- profile_init: float32 [2, 512], replicated, may hold values from -1.4 to 1.4
Outputs:
- filter_out: float32 [2, 32768], P(None, 'chan')
- profile_out: float32 [2, 512], replicated
- misfit: float32 [1], replicated
The draws below stay inside these ranges and needn't reach their ends.
All inputs are finite; a program needn't handle non-finite values.
Results may differ from the reference program's by a relative error of at most 0.0003.
Values sent between devices are 32-bit elements; how exact they have to be, the bound alone decides.
A program may use at most 192 MiB of HBM per device.

```python
import jax
import jax.numpy as jnp
from jax import lax

CHANNELS = 32768
HARM = 512
ITERS = 1
SUBS = 4


def draw_start(key):
    subkeys = jax.random.split(jax.random.fold_in(key, 5), 2)
    filt = jnp.clip(0.7 * jax.random.normal(subkeys[0], (2, CHANNELS), jnp.float32), -2.1, 2.1)
    prof = jnp.clip(0.7 * jax.random.normal(subkeys[1], (2, HARM), jnp.float32), -1.4, 1.4)
    return (filt, prof)


def draw_filter_init(key, part):
    return draw_start(key)[0].astype(jnp.float32)


def draw_profile_init(key, part):
    return draw_start(key)[1].astype(jnp.float32)


def start_model(filt, prof):
    padded = jnp.pad(filt, ((0, 0), (HARM, HARM)))

    def one_row(harmonic):
        forward = lax.dynamic_slice_in_dim(padded, HARM + harmonic, CHANNELS, 1)
        backward = lax.dynamic_slice_in_dim(padded, HARM - harmonic, CHANNELS, 1)
        prod_re = forward[0] * backward[0] + forward[1] * backward[1]
        prod_im = forward[1] * backward[0] - forward[0] * backward[1]
        prof_re = prof[0, harmonic]
        prof_im = prof[1, harmonic]
        return jnp.stack([prod_re * prof_re - prod_im * prof_im, prod_re * prof_im + prod_im * prof_re])
    rows = jax.vmap(one_row)(jnp.arange(HARM).astype(jnp.int32))
    return jnp.transpose(rows, (1, 0, 2))


def draw_spectra(key, part):
    filt, prof = draw_start(key)
    model = start_model(filt, prof)
    subkeys = jax.random.split(jax.random.fold_in(key, 11), 1)
    channel_pos = jnp.arange(CHANNELS).astype(jnp.float32) / CHANNELS
    sub_pos = jnp.arange(SUBS).astype(jnp.float32) / SUBS
    levels = (0.4 + 0.8 * channel_pos)[None, None, None, :] * (0.7 + 0.6 * sub_pos)[:, None, None, None]
    noise = jax.random.normal(subkeys[0], (SUBS, 2, HARM, CHANNELS), jnp.float32) * levels
    values = model[None] + 0.5 * noise
    return jnp.clip(values, -12.0, 12.0).astype(jnp.bfloat16)


def setup_inputs(seed: int = 0) -> dict:
    arg_keys = jax.random.split(jax.random.key(seed), 4)
    return {
        "spectra": draw_spectra(jax.random.fold_in(arg_keys[3], 71), 0),
        "filter_init": draw_filter_init(jax.random.fold_in(arg_keys[3], 71), 0),
        "profile_init": draw_profile_init(jax.random.fold_in(arg_keys[3], 71), 0),
    }


filter_rate = 0.1
profile_rate = 0.1
epsilon = 1e-06

def energy(filt, prof, spectrum):
    padded = jnp.pad(filt, ((0, 0), (HARM, HARM)))
    channel_idx = jnp.arange(CHANNELS).astype(jnp.int32)[None, :]
    harmonic_idx = jnp.arange(HARM).astype(jnp.int32)[:, None]
    forward = padded[:, HARM + channel_idx + harmonic_idx]
    backward = padded[:, HARM + channel_idx - harmonic_idx]
    prod_re = forward[0] * backward[0] + forward[1] * backward[1]
    prod_im = forward[1] * backward[0] - forward[0] * backward[1]
    prof_re = prof[0][:, None]
    prof_im = prof[1][:, None]
    model_re = prod_re * prof_re - prod_im * prof_im
    model_im = prod_re * prof_im + prod_im * prof_re
    resid_re = spectrum[0] - model_re
    resid_im = spectrum[1] - model_im
    return jnp.sum(resid_re * resid_re + resid_im * resid_im)

def reference(spectra, filter_init, profile_init):
    norm_scale = 1.0 / (SUBS * HARM)
    filt = filter_init
    prof = profile_init
    misfits = []
    for iteration in range(ITERS):

        def accumulate(totals, spectrum):
            energy_value, grads = jax.value_and_grad(energy, argnums=(0, 1))(filt, prof, spectrum.astype(jnp.float32))
            return ((totals[0] + energy_value, totals[1] + grads[0], totals[2] + grads[1]), None)
        start_sums = (jnp.zeros((), jnp.float32), jnp.zeros_like(filt), jnp.zeros_like(prof))
        totals, unused = lax.scan(accumulate, start_sums, spectra)
        error = totals[0] * norm_scale
        filter_grad = totals[1] * norm_scale
        profile_grad = totals[2] * norm_scale
        misfits.append(error / CHANNELS)
        filt = filt - filter_rate * filter_grad / jnp.sqrt(jnp.sum(filter_grad * filter_grad) / (2 * CHANNELS) + epsilon)
        prof = prof - profile_rate * profile_grad / jnp.sqrt(jnp.mean(profile_grad * profile_grad) + epsilon)
    return (filt, prof, jnp.stack(misfits))
```

```python
import functools

import jax
import jax.numpy as jnp
from jax import lax
from jax.experimental import pallas as pl
from jax.experimental.pallas import tpu as pltpu
from jax.sharding import PartitionSpec as P

filter_rate = 0.1
profile_rate = 0.1
epsilon = 1e-06
LANES = 128
MESH = pl.DeviceIdType.MESH
F32 = jnp.float32


def lanes_of(shape):
    return lax.broadcasted_iota(jnp.int32, shape, len(shape) - 1)


def shift_right(x, k):
    rolled = pltpu.roll(x, k, 2)
    before = jnp.concatenate([rolled[-1:], rolled[:-1]], axis=0)
    return jnp.where(lanes_of(x.shape) >= k, rolled, before)


def shift_left(x, k):
    rolled = pltpu.roll(x, LANES - k, 2)
    after = jnp.concatenate([rolled[1:], rolled[:1]], axis=0)
    return jnp.where(lanes_of(x.shape) < LANES - k, rolled, after)


def by_sublane(x, shift):
    sub = lax.broadcasted_iota(jnp.int32, x.shape, 1)
    for k in (1, 2, 4):
        x = jnp.where((sub & k) != 0, shift(x, k), x)
    return x


def gradient_kernel(
    nb, na, factor, f_ref, q_ref, x_ref, main_ref, tail_ref, head_ref,
    base_f, base_b, fwd, bwd, up, lo, up_all, lo_all, prof_acc, err_acc,
):
    m = pl.program_id(0)
    ext = nb + na
    tile = (8, LANES)

    @pl.when(m == 0)
    def _():
        for ri in range(2):
            high = jnp.broadcast_to(f_ref[ri, na:, :][:, None, :], (ext, 8, LANES))
            base_f[ri] = by_sublane(high, shift_left)
            low = jnp.broadcast_to(f_ref[ri, :ext, :][:, None, :], (ext, 8, LANES))
            base_b[ri] = by_sublane(low, shift_right)
        up_all[...] = jnp.zeros_like(up_all)
        lo_all[...] = jnp.zeros_like(lo_all)
        err_acc[...] = jnp.zeros_like(err_acc)

    lane = lanes_of(tile)
    for g in range(2):
        t = 16 * m + 8 * g
        left = lax.rem(LANES - t, LANES)
        rows = slice(8 * g, 8 * g + 8)
        for ri in range(2):
            now = pltpu.roll(base_f[ri, 0], left, 1)
            for n in range(ext - 1):
                after = pltpu.roll(base_f[ri, n + 1], left, 1)
                fwd[ri, n, rows] = jnp.where(lane < LANES - t, now, after)
                now = after
            before = pltpu.roll(base_b[ri, 0], t, 1)
            for n in range(1, ext):
                now = pltpu.roll(base_b[ri, n], t, 1)
                bwd[ri, n, rows] = jnp.where(lane >= t, now, before)
                before = now

    for ri in range(2):
        for n in range(na - 1):
            up[ri, nb + n] = jnp.zeros((16, LANES), F32)
            lo[ri, n] = jnp.zeros((16, LANES), F32)

    for a in range(na):
        qr = q_ref[0, a]
        qi = q_ref[1, a]

        def body(b, carry, a=a, qr=qr, qi=qi):
            gr, gi, er = carry
            cols = pl.ds(pl.multiple_of(b * LANES, LANES), LANES)
            xr = x_ref[0, a, :, cols].astype(F32)
            xi = x_ref[1, a, :, cols].astype(F32)
            fr, fi = fwd[0, b + a], fwd[1, b + a]
            br, bi = bwd[0, b - a + na], bwd[1, b - a + na]
            pr = fr * br + fi * bi
            pi = fi * br - fr * bi
            rr = xr - (pr * qr - pi * qi)
            ri = xi - (pr * qi + pi * qr)
            er = er + (rr * rr + ri * ri)
            gr = gr + (rr * pr + ri * pi)
            gi = gi + (ri * pr - rr * pi)
            yr = rr * qr + ri * qi
            yi = ri * qr - rr * qi
            ur = yr * br - yi * bi
            ui = yr * bi + yi * br
            vr = yr * fr + yi * fi
            vi = yr * fi - yi * fr
            iu, il = b + a, b - a + na - 1
            if a == 0:
                up[0, iu] = ur
                up[1, iu] = ui
                lo[0, il] = vr
                lo[1, il] = vi
            else:
                up[0, iu] = up[0, iu] + ur
                up[1, iu] = up[1, iu] + ui
                lo[0, il] = lo[0, il] + vr
                lo[1, il] = lo[1, il] + vi
            return gr, gi, er

        zero = jnp.zeros((16, LANES), F32)
        gr, gi, er = lax.fori_loop(0, nb, body, (zero, zero, zero), unroll=2)
        rows = pl.ds(pl.multiple_of(16 * m, 16), 16)
        prof_acc[0, a, rows] = gr
        prof_acc[1, a, rows] = gi
        err_acc[...] = err_acc[...] + er

    zero8 = jnp.zeros(tile, F32)
    for g in range(2):
        t = 16 * m + 8 * g
        left = lax.rem(LANES - t, LANES)
        rows = slice(8 * g, 8 * g + 8)
        for ri in range(2):
            before = zero8
            for n in range(ext):
                now = pltpu.roll(up[ri, n, rows], t, 1) if n < ext - 1 else zero8
                up_all[ri, n] = up_all[ri, n] + jnp.where(lane >= t, now, before)
                before = now
            before = zero8
            for n in range(ext):
                now = pltpu.roll(lo[ri, n, rows], left, 1) if n < ext - 1 else zero8
                lo_all[ri, n] = lo_all[ri, n] + jnp.where(lane < LANES - t, before, now)
                before = now

    @pl.when(m == pl.num_programs(0) - 1)
    def _():
        for ri in range(2):
            upper = factor * jnp.sum(by_sublane(up_all[ri], shift_right), axis=1)
            lower = factor * jnp.sum(by_sublane(lo_all[ri], shift_left), axis=1)
            main_ref[ri * nb : (ri + 1) * nb] = upper[:nb] + lower[na:]
            tail_ref[ri * na : (ri + 1) * na] = upper[nb:]
            head_ref[ri * na : (ri + 1) * na] = lower[:na]
            for a in range(na):
                sums = lax.dot_general(
                    jnp.ones(tile, F32), prof_acc[ri, a], (((1,), (1,)), ((), ())),
                    precision=lax.Precision.HIGHEST, preferred_element_type=F32,
                )
                row = 2 * nb + ri * na + a
                main_ref[row : row + 1] = factor * sums[:1]
        main_ref[2 * nb + 2 * na : 2 * nb + 2 * na + 1] = jnp.sum(
            err_acc[...], axis=0, keepdims=True
        )


def reduce_kernel(
    nb, na, n_chan, n_sub, harmonics, weight, f_ref, q_ref, main_ref, tail_ref, head_ref,
    out_ref, prof_ref, misfit_ref,
    mains, tails, heads, packs, pack,
    s_main, r_main, s_tail, r_tail, s_head, r_head, s_pack, r_pack,
):
    chan = lax.axis_index("chan")
    sub = lax.axis_index("sub")
    above = lax.rem(chan + 1, n_chan)
    below = lax.rem(chan + n_chan - 1, n_chan)

    barrier = pltpu.get_barrier_semaphore()
    greeted = 0
    for off in range(n_sub):
        peer = lax.rem(sub + off, n_sub)
        for c in (above, below) + ((chan,) if off else ()):
            pl.semaphore_signal(barrier, inc=1, device_id=(c, peer), device_id_type=MESH)
            greeted += 1
    for off in range(2, n_chan - 1):
        pl.semaphore_signal(
            barrier, inc=1, device_id=(lax.rem(chan + off, n_chan), sub), device_id_type=MESH
        )
        greeted += 1
    pl.semaphore_wait(barrier, greeted)

    def copy_to(src, dst, send, recv, device):
        return pltpu.make_async_remote_copy(
            src_ref=src, dst_ref=dst, send_sem=send, recv_sem=recv,
            device_id=device, device_id_type=MESH,
        )

    sends = []
    for off in range(1, n_sub):
        peer = lax.rem(sub + off, n_sub)
        sends.append(
            copy_to(main_ref, mains.at[sub], s_main.at[off], r_main.at[sub], (chan, peer))
        )
    for off in range(n_sub):
        peer = lax.rem(sub + off, n_sub)
        sends.append(
            copy_to(tail_ref, tails.at[sub], s_tail.at[off], r_tail.at[sub], (above, peer))
        )
        sends.append(
            copy_to(head_ref, heads.at[sub], s_head.at[off], r_head.at[sub], (below, peer))
        )
    for copy in sends:
        copy.start()
    mains[sub] = main_ref[...]
    for off in range(n_sub):
        peer = lax.rem(sub + off, n_sub)
        if off:
            copy_to(
                main_ref, mains.at[peer], s_main.at[off], r_main.at[peer], (chan, peer)
            ).wait_recv()
        copy_to(
            tail_ref, tails.at[peer], s_tail.at[off], r_tail.at[peer], (above, peer)
        ).wait_recv()
        copy_to(
            head_ref, heads.at[peer], s_head.at[off], r_head.at[peer], (below, peer)
        ).wait_recv()

    total = mains[0]
    tail = tails[0]
    head = heads[0]
    for s in range(1, n_sub):
        total = total + mains[s]
        tail = tail + tails[s]
        head = head + heads[s]
    tail = jnp.where(chan > 0, tail, 0.0)
    head = jnp.where(chan < n_chan - 1, head, 0.0)
    grads = []
    squares = jnp.zeros((1, LANES), F32)
    for ri in range(2):
        own = total[ri * nb : (ri + 1) * nb]
        part = slice(ri * na, (ri + 1) * na)
        grad = jnp.concatenate([own[:na] + tail[part], own[na:]], axis=0)
        grad = jnp.concatenate([grad[: nb - na], grad[nb - na :] + head[part]], axis=0)
        squares = squares + jnp.sum(grad * grad, axis=0, keepdims=True)
        grads.append(grad)
    prof_rows = 2 * na
    pack[...] = jnp.zeros_like(pack)
    pack[: prof_rows + 1] = total[2 * nb : 2 * nb + prof_rows + 1]
    pack[prof_rows + 1 : prof_rows + 2] = squares
    packs[chan] = pack[...]

    for copy in sends:
        copy.wait_send()
    exchanges = []
    for off in range(1, n_chan):
        peer = lax.rem(chan + off, n_chan)
        exchanges.append(
            copy_to(pack, packs.at[chan], s_pack.at[off], r_pack.at[chan], (peer, sub))
        )
    for copy in exchanges:
        copy.start()
    for off in range(1, n_chan):
        peer = lax.rem(chan + off, n_chan)
        copy_to(pack, packs.at[peer], s_pack.at[off], r_pack.at[peer], (peer, sub)).wait_recv()
    sums = packs[0]
    for c in range(1, n_chan):
        sums = sums + packs[c]
    prof_grad = sums[:prof_rows]
    error = jnp.sum(sums[prof_rows : prof_rows + 1])
    square = jnp.sum(sums[prof_rows + 1 : prof_rows + 2], axis=1, keepdims=True)
    channels = n_chan * nb * LANES
    misfit_ref[0] = error * (weight / channels)
    scale = filter_rate / jnp.sqrt(square / (2 * channels) + epsilon)
    for ri in range(2):
        step = grads[ri] * scale
        for n in range(nb):
            cols = slice(n * LANES, (n + 1) * LANES)
            out_ref[ri : ri + 1, cols] = f_ref[ri : ri + 1, cols] - step[n : n + 1]
    mean = jnp.sum(prof_grad * prof_grad, keepdims=True) / (2 * harmonics)
    prof_step = prof_grad * (profile_rate / jnp.sqrt(mean + epsilon))
    for ri in range(2):
        for a in range(na):
            cols = slice(a * LANES, (a + 1) * LANES)
            row = ri * na + a
            prof_ref[ri : ri + 1, cols] = q_ref[ri : ri + 1, cols] - prof_step[row : row + 1]
    for copy in exchanges:
        copy.wait_send()


def on_device(spectra, filter_init, profile_init):
    harmonics = profile_init.shape[1]
    owned = filter_init.shape[1]
    n_chan = lax.axis_size("chan")
    n_sub = lax.axis_size("sub")
    nb = owned // LANES
    na = harmonics // LANES
    ext = nb + na
    weight = 1.0 / (n_sub * spectra.shape[0] * harmonics)
    factor = -2.0 * weight
    main_rows = 2 * nb + 2 * na + 8

    low = lax.ppermute(
        filter_init[:, owned - harmonics :], "chan", [(i, i + 1) for i in range(n_chan - 1)]
    )
    high = lax.ppermute(
        filter_init[:, :harmonics], "chan", [(i + 1, i) for i in range(n_chan - 1)]
    )
    padded = jnp.concatenate([low, filter_init, high], axis=1).reshape(2, nb + 2 * na, LANES)
    prof = jnp.broadcast_to(
        profile_init.reshape(2, na, LANES)[..., None], (2, na, LANES, LANES)
    )
    x = spectra.reshape(2, na, LANES, owned)

    whole = pl.BlockSpec(memory_space=pltpu.VMEM)
    main, tail, head = pl.pallas_call(
        functools.partial(gradient_kernel, nb, na, factor),
        grid=(LANES // 16,),
        in_specs=[
            pl.BlockSpec((2, nb + 2 * na, LANES), lambda m: (0, 0, 0)),
            pl.BlockSpec((2, na, 16, LANES), lambda m: (0, 0, m, 0)),
            pl.BlockSpec((2, na, 16, owned), lambda m: (0, 0, m, 0)),
        ],
        out_specs=[
            pl.BlockSpec((main_rows, LANES), lambda m: (0, 0)),
            pl.BlockSpec((2 * na, LANES), lambda m: (0, 0)),
            pl.BlockSpec((2 * na, LANES), lambda m: (0, 0)),
        ],
        out_shape=[
            jax.ShapeDtypeStruct((main_rows, LANES), F32),
            jax.ShapeDtypeStruct((2 * na, LANES), F32),
            jax.ShapeDtypeStruct((2 * na, LANES), F32),
        ],
        scratch_shapes=[
            pltpu.VMEM((2, ext, 8, LANES), F32),
            pltpu.VMEM((2, ext, 8, LANES), F32),
            pltpu.VMEM((2, ext, 16, LANES), F32),
            pltpu.VMEM((2, ext, 16, LANES), F32),
            pltpu.VMEM((2, ext, 16, LANES), F32),
            pltpu.VMEM((2, ext, 16, LANES), F32),
            pltpu.VMEM((2, ext, 8, LANES), F32),
            pltpu.VMEM((2, ext, 8, LANES), F32),
            pltpu.VMEM((2, na, LANES, LANES), F32),
            pltpu.VMEM((16, LANES), F32),
        ],
    )(padded, prof, x)

    dma = pltpu.SemaphoreType.DMA
    return pl.pallas_call(
        functools.partial(reduce_kernel, nb, na, n_chan, n_sub, harmonics, weight),
        in_specs=[whole] * 5,
        out_specs=[whole, whole, pl.BlockSpec(memory_space=pltpu.SMEM)],
        out_shape=[
            jax.ShapeDtypeStruct((2, owned), F32),
            jax.ShapeDtypeStruct((2, harmonics), F32),
            jax.ShapeDtypeStruct((1,), F32),
        ],
        scratch_shapes=[
            pltpu.VMEM((n_sub, main_rows, LANES), F32),
            pltpu.VMEM((n_sub, 2 * na, LANES), F32),
            pltpu.VMEM((n_sub, 2 * na, LANES), F32),
            pltpu.VMEM((n_chan, 2 * na + 8, LANES), F32),
            pltpu.VMEM((2 * na + 8, LANES), F32),
            dma((n_sub,)), dma((n_sub,)),
            dma((n_sub,)), dma((n_sub,)),
            dma((n_sub,)), dma((n_sub,)),
            dma((n_chan,)), dma((n_chan,)),
        ],
        compiler_params=pltpu.CompilerParams(collective_id=0, has_side_effects=True),
    )(filter_init, profile_init, main, tail, head)


def solution(mesh):
    return jax.shard_map(
        on_device,
        mesh=mesh,
        in_specs=(P("sub", None, None, "chan"), P(None, "chan"), P()),
        out_specs=(P(None, "chan"), P(), P()),
        check_vma=False,
    )
```

```python
import functools

import jax
import jax.numpy as jnp
from jax import lax
from jax.experimental import pallas as pl
from jax.experimental.pallas import tpu as pltpu
from jax.sharding import PartitionSpec as P

filter_rate = 0.1
profile_rate = 0.1
epsilon = 1e-06
LANES = 128
MESH = pl.DeviceIdType.MESH
F32 = jnp.float32


def lanes_of(shape):
    return lax.broadcasted_iota(jnp.int32, shape, len(shape) - 1)


def shift_right(x, k):
    rolled = pltpu.roll(x, k, 2)
    before = jnp.concatenate([rolled[-1:], rolled[:-1]], axis=0)
    return jnp.where(lanes_of(x.shape) >= k, rolled, before)


def shift_left(x, k):
    rolled = pltpu.roll(x, LANES - k, 2)
    after = jnp.concatenate([rolled[1:], rolled[:1]], axis=0)
    return jnp.where(lanes_of(x.shape) < LANES - k, rolled, after)


def by_sublane(x, shift):
    sub = lax.broadcasted_iota(jnp.int32, x.shape, 1)
    for k in (1, 2, 4):
        x = jnp.where((sub & k) != 0, shift(x, k), x)
    return x


def halo_kernel(nb, na, n_chan, f_ref, q_ref, pad_ref, prof_ref, low, high, s_sem, r_sem):
    chan = lax.axis_index("chan")
    sub = lax.axis_index("sub")
    above = lax.rem(chan + 1, n_chan)
    below = lax.rem(chan + n_chan - 1, n_chan)
    width = na * LANES
    owned = nb * LANES
    barrier = pltpu.get_barrier_semaphore()
    for c in (above, below):
        pl.semaphore_signal(barrier, inc=1, device_id=(c, sub), device_id_type=MESH)
    pl.semaphore_wait(barrier, 2)
    copies = [
        pltpu.make_async_remote_copy(
            src_ref=f_ref.at[:, pl.ds(start, width)], dst_ref=dst, send_sem=s_sem.at[i],
            recv_sem=r_sem.at[i], device_id=(c, sub), device_id_type=MESH,
        )
        for i, (start, dst, c) in enumerate(((owned - width, low, above), (0, high, below)))
    ]
    for copy in copies:
        copy.start()
    for ri in range(2):
        for n in range(nb):
            pad_ref[ri, na + n : na + n + 1] = f_ref[ri : ri + 1, n * LANES : (n + 1) * LANES]
        for a in range(na):
            row = q_ref[ri : ri + 1, a * LANES : (a + 1) * LANES]
            prof_ref[ri, a] = jnp.broadcast_to(row, (LANES, LANES)).T
    for copy in copies:
        copy.wait()
    has_low = chan > 0
    has_high = chan < n_chan - 1
    for ri in range(2):
        for n in range(na):
            cols = slice(n * LANES, (n + 1) * LANES)
            pad_ref[ri, n : n + 1] = jnp.where(has_low, low[ri : ri + 1, cols], 0.0)
            row = na + nb + n
            pad_ref[ri, row : row + 1] = jnp.where(has_high, high[ri : ri + 1, cols], 0.0)


def gradient_kernel(
    nb, na, factor, f_ref, q_ref, x_ref, main_ref, tail_ref, head_ref,
    base_f, base_b, fwd, bwd, up, lo, up_all, lo_all, prof_acc, err_acc,
):
    m = pl.program_id(0)
    last = pl.num_programs(0) - 1
    ext = nb + na
    tile = (8, LANES)
    pairs = [(ri, g) for ri in range(2) for g in range(2)]
    lane = lanes_of(tile)
    zero8 = jnp.zeros(tile, F32)

    def rows(g):
        return slice(8 * g, 8 * g + 8)

    def shifts(step):
        right = [lax.rem(16 * step + 8 * g, LANES) for g in range(2)]
        left = [lax.rem(LANES - t, LANES) for t in right]
        keep_right = [lane >= t for t in right]
        keep_left = [lane < LANES - t for t in right]
        return right, left, keep_right, keep_left

    def build_fwd(step):
        _, left, _, keep = shifts(step)
        slot = lax.rem(step, 2)
        init = tuple(pltpu.roll(base_f[ri, 0], left[g], 1) for ri, g in pairs)

        def one(n, carry):
            out = []
            for (ri, g), now in zip(pairs, carry):
                after = pltpu.roll(base_f[ri, n + 1], left[g], 1)
                fwd[slot, ri, n, rows(g)] = jnp.where(keep[g], now, after)
                out.append(after)
            return tuple(out)

        return init, one, ext - 1

    def build_bwd(step):
        right, _, keep, _ = shifts(step)
        slot = lax.rem(step, 2)
        init = tuple(pltpu.roll(base_b[ri, 0], right[g], 1) for ri, g in pairs)

        def one(n, carry):
            out = []
            for (ri, g), before in zip(pairs, carry):
                now = pltpu.roll(base_b[ri, n + 1], right[g], 1)
                bwd[slot, ri, n + 1, rows(g)] = jnp.where(keep[g], now, before)
                out.append(now)
            return tuple(out)

        return init, one, ext - 1

    def add_shifted(total, parts, shift, pick):
        def run(step, slot):
            amount, keep = shift(step)
            init = (zero8,) * 4

            def one(n, carry):
                out = []
                sums = [total[ri, n] for ri in range(2)]
                for (ri, g), before in zip(pairs, carry):
                    now = pltpu.roll(parts[slot, ri, n, rows(g)], amount[g], 1)
                    sums[ri] = sums[ri] + pick(keep[g], now, before)
                    out.append(now)
                for ri in range(2):
                    total[ri, n] = sums[ri]
                return tuple(out)

            return init, one, ext

        return run

    def right_of(step):
        right, _, keep, _ = shifts(step)
        return right, keep

    def left_of(step):
        _, left, _, keep = shifts(step)
        return left, keep

    shear_up = add_shifted(up_all, up, right_of, lambda k, now, before: jnp.where(k, now, before))
    shear_lo = add_shifted(lo_all, lo, left_of, lambda k, now, before: jnp.where(k, before, now))

    def run_all(task):
        init, one, count = task
        for n in range(count):
            init = one(n, init)

    slot = lax.rem(m, 2)
    other = lax.rem(m + 1, 2)

    @pl.when(m == 0)
    def _():
        for ri in range(2):
            high = jnp.broadcast_to(f_ref[ri, na:, :][:, None, :], (ext, 8, LANES))
            base_f[ri] = by_sublane(high, shift_left)
            low = jnp.broadcast_to(f_ref[ri, :ext, :][:, None, :], (ext, 8, LANES))
            base_b[ri] = by_sublane(low, shift_right)
        up_all[...] = jnp.zeros_like(up_all)
        lo_all[...] = jnp.zeros_like(lo_all)
        up[...] = jnp.zeros_like(up)
        lo[...] = jnp.zeros_like(lo)
        err_acc[...] = jnp.zeros_like(err_acc)
        run_all(build_fwd(m))
        run_all(build_bwd(m))

    for ri in range(2):
        for n in range(na - 1):
            up[slot, ri, nb + n] = jnp.zeros((16, LANES), F32)
            lo[slot, ri, n] = jnp.zeros((16, LANES), F32)

    tasks = [
        build_fwd(m + 1), build_bwd(m + 1), shear_up(m + last, other), shear_lo(m + last, other)
    ]
    for a in range(na):
        qr = q_ref[0, a]
        qi = q_ref[1, a]
        init, side, count = tasks[a] if a < 4 else ((), lambda n, carry: carry, 0)

        def body(b, carry, a=a, qr=qr, qi=qi, side=side):
            gr, gi, er, beside = carry
            cols = pl.ds(pl.multiple_of(b * LANES, LANES), LANES)
            xr = x_ref[0, a, :, cols].astype(F32)
            xi = x_ref[1, a, :, cols].astype(F32)
            fr, fi = fwd[slot, 0, b + a], fwd[slot, 1, b + a]
            br, bi = bwd[slot, 0, b - a + na], bwd[slot, 1, b - a + na]
            beside = side(b, beside)
            pr = fr * br + fi * bi
            pi = fi * br - fr * bi
            rr = xr - (pr * qr - pi * qi)
            ri = xi - (pr * qi + pi * qr)
            er = er + (rr * rr + ri * ri)
            gr = gr + (rr * pr + ri * pi)
            gi = gi + (ri * pr - rr * pi)
            yr = rr * qr + ri * qi
            yi = ri * qr - rr * qi
            ur = yr * br - yi * bi
            ui = yr * bi + yi * br
            vr = yr * fr + yi * fi
            vi = yr * fi - yi * fr
            iu, il = b + a, b - a + na - 1
            if a == 0:
                up[slot, 0, iu] = ur
                up[slot, 1, iu] = ui
                lo[slot, 0, il] = vr
                lo[slot, 1, il] = vi
            else:
                up[slot, 0, iu] = up[slot, 0, iu] + ur
                up[slot, 1, iu] = up[slot, 1, iu] + ui
                lo[slot, 0, il] = lo[slot, 0, il] + vr
                lo[slot, 1, il] = lo[slot, 1, il] + vi
            return gr, gi, er, beside

        zero = jnp.zeros((16, LANES), F32)
        gr, gi, er, beside = lax.fori_loop(0, nb, body, (zero, zero, zero, init), unroll=2)
        for n in range(nb, count):
            beside = side(n, beside)
        group = pl.ds(pl.multiple_of(16 * m, 16), 16)
        prof_acc[0, a, group] = gr
        prof_acc[1, a, group] = gi
        err_acc[...] = err_acc[...] + er
    for task in tasks[na:]:
        run_all(task)

    @pl.when(m == last)
    def _():
        run_all(shear_up(m, slot))
        run_all(shear_lo(m, slot))
        for ri in range(2):
            upper = factor * jnp.sum(by_sublane(up_all[ri], shift_right), axis=1)
            lower = factor * jnp.sum(by_sublane(lo_all[ri], shift_left), axis=1)
            main_ref[ri * nb : (ri + 1) * nb] = upper[:nb] + lower[na:]
            tail_ref[ri * na : (ri + 1) * na] = upper[nb:]
            head_ref[ri * na : (ri + 1) * na] = lower[:na]
            for a in range(na):
                sums = lax.dot_general(
                    jnp.ones(tile, F32), prof_acc[ri, a], (((1,), (1,)), ((), ())),
                    precision=lax.Precision.HIGHEST, preferred_element_type=F32,
                )
                row = 2 * nb + ri * na + a
                main_ref[row : row + 1] = factor * sums[:1]
        main_ref[2 * nb + 2 * na : 2 * nb + 2 * na + 1] = jnp.sum(
            err_acc[...], axis=0, keepdims=True
        )


def reduce_kernel(
    nb, na, n_chan, n_sub, harmonics, weight, f_ref, q_ref, main_ref, tail_ref, head_ref,
    out_ref, prof_ref, misfit_ref,
    mains, tails, heads, packs, pack,
    s_main, r_main, s_tail, r_tail, s_head, r_head, s_pack, r_pack,
):
    chan = lax.axis_index("chan")
    sub = lax.axis_index("sub")
    above = lax.rem(chan + 1, n_chan)
    below = lax.rem(chan + n_chan - 1, n_chan)

    barrier = pltpu.get_barrier_semaphore()
    greeted = 0
    for off in range(n_sub):
        peer = lax.rem(sub + off, n_sub)
        for c in (above, below) + ((chan,) if off else ()):
            pl.semaphore_signal(barrier, inc=1, device_id=(c, peer), device_id_type=MESH)
            greeted += 1
    for off in range(2, n_chan - 1):
        pl.semaphore_signal(
            barrier, inc=1, device_id=(lax.rem(chan + off, n_chan), sub), device_id_type=MESH
        )
        greeted += 1
    pl.semaphore_wait(barrier, greeted)

    def copy_to(src, dst, send, recv, device):
        return pltpu.make_async_remote_copy(
            src_ref=src, dst_ref=dst, send_sem=send, recv_sem=recv,
            device_id=device, device_id_type=MESH,
        )

    sends = []
    for off in range(1, n_sub):
        peer = lax.rem(sub + off, n_sub)
        sends.append(
            copy_to(main_ref, mains.at[sub], s_main.at[off], r_main.at[sub], (chan, peer))
        )
    for off in range(n_sub):
        peer = lax.rem(sub + off, n_sub)
        sends.append(
            copy_to(tail_ref, tails.at[sub], s_tail.at[off], r_tail.at[sub], (above, peer))
        )
        sends.append(
            copy_to(head_ref, heads.at[sub], s_head.at[off], r_head.at[sub], (below, peer))
        )
    for copy in sends:
        copy.start()
    mains[sub] = main_ref[...]
    for off in range(n_sub):
        peer = lax.rem(sub + off, n_sub)
        if off:
            copy_to(
                main_ref, mains.at[peer], s_main.at[off], r_main.at[peer], (chan, peer)
            ).wait_recv()
        copy_to(
            tail_ref, tails.at[peer], s_tail.at[off], r_tail.at[peer], (above, peer)
        ).wait_recv()
        copy_to(
            head_ref, heads.at[peer], s_head.at[off], r_head.at[peer], (below, peer)
        ).wait_recv()

    total = mains[0]
    tail = tails[0]
    head = heads[0]
    for s in range(1, n_sub):
        total = total + mains[s]
        tail = tail + tails[s]
        head = head + heads[s]
    tail = jnp.where(chan > 0, tail, 0.0)
    head = jnp.where(chan < n_chan - 1, head, 0.0)
    grads = []
    squares = jnp.zeros((1, LANES), F32)
    for ri in range(2):
        own = total[ri * nb : (ri + 1) * nb]
        part = slice(ri * na, (ri + 1) * na)
        grad = jnp.concatenate([own[:na] + tail[part], own[na:]], axis=0)
        grad = jnp.concatenate([grad[: nb - na], grad[nb - na :] + head[part]], axis=0)
        squares = squares + jnp.sum(grad * grad, axis=0, keepdims=True)
        grads.append(grad)
    prof_rows = 2 * na
    pack[...] = jnp.zeros_like(pack)
    pack[: prof_rows + 1] = total[2 * nb : 2 * nb + prof_rows + 1]
    pack[prof_rows + 1 : prof_rows + 2] = squares
    packs[chan] = pack[...]

    for copy in sends:
        copy.wait_send()
    exchanges = []
    for off in range(1, n_chan):
        peer = lax.rem(chan + off, n_chan)
        exchanges.append(
            copy_to(pack, packs.at[chan], s_pack.at[off], r_pack.at[chan], (peer, sub))
        )
    for copy in exchanges:
        copy.start()
    for off in range(1, n_chan):
        peer = lax.rem(chan + off, n_chan)
        copy_to(pack, packs.at[peer], s_pack.at[off], r_pack.at[peer], (peer, sub)).wait_recv()
    sums = packs[0]
    for c in range(1, n_chan):
        sums = sums + packs[c]
    prof_grad = sums[:prof_rows]
    error = jnp.sum(sums[prof_rows : prof_rows + 1])
    square = jnp.sum(sums[prof_rows + 1 : prof_rows + 2], axis=1, keepdims=True)
    channels = n_chan * nb * LANES
    misfit_ref[0] = error * (weight / channels)
    scale = filter_rate / jnp.sqrt(square / (2 * channels) + epsilon)
    for ri in range(2):
        step = grads[ri] * scale
        for n in range(nb):
            cols = slice(n * LANES, (n + 1) * LANES)
            out_ref[ri : ri + 1, cols] = f_ref[ri : ri + 1, cols] - step[n : n + 1]
    mean = jnp.sum(prof_grad * prof_grad, keepdims=True) / (2 * harmonics)
    prof_step = prof_grad * (profile_rate / jnp.sqrt(mean + epsilon))
    for ri in range(2):
        for a in range(na):
            cols = slice(a * LANES, (a + 1) * LANES)
            row = ri * na + a
            prof_ref[ri : ri + 1, cols] = q_ref[ri : ri + 1, cols] - prof_step[row : row + 1]
    for copy in exchanges:
        copy.wait_send()


def on_device(spectra, filter_init, profile_init):
    harmonics = profile_init.shape[1]
    owned = filter_init.shape[1]
    n_chan = lax.axis_size("chan")
    n_sub = lax.axis_size("sub")
    nb = owned // LANES
    na = harmonics // LANES
    ext = nb + na
    weight = 1.0 / (n_sub * spectra.shape[0] * harmonics)
    factor = -2.0 * weight
    main_rows = 2 * nb + 2 * na + 8

    whole = pl.BlockSpec(memory_space=pltpu.VMEM)
    dma = pltpu.SemaphoreType.DMA
    padded, prof = pl.pallas_call(
        functools.partial(halo_kernel, nb, na, n_chan),
        in_specs=[whole] * 2,
        out_specs=[whole] * 2,
        out_shape=[
            jax.ShapeDtypeStruct((2, nb + 2 * na, LANES), F32),
            jax.ShapeDtypeStruct((2, na, LANES, LANES), F32),
        ],
        scratch_shapes=[
            pltpu.VMEM((2, harmonics), F32), pltpu.VMEM((2, harmonics), F32), dma((2,)), dma((2,)),
        ],
        compiler_params=pltpu.CompilerParams(collective_id=1, has_side_effects=True),
    )(filter_init, profile_init)
    x = spectra.reshape(2, na, LANES, owned)

    main, tail, head = pl.pallas_call(
        functools.partial(gradient_kernel, nb, na, factor),
        grid=(LANES // 16,),
        in_specs=[
            pl.BlockSpec((2, nb + 2 * na, LANES), lambda m: (0, 0, 0)),
            pl.BlockSpec((2, na, 16, LANES), lambda m: (0, 0, m, 0)),
            pl.BlockSpec((2, na, 16, owned), lambda m: (0, 0, m, 0)),
        ],
        out_specs=[
            pl.BlockSpec((main_rows, LANES), lambda m: (0, 0)),
            pl.BlockSpec((2 * na, LANES), lambda m: (0, 0)),
            pl.BlockSpec((2 * na, LANES), lambda m: (0, 0)),
        ],
        out_shape=[
            jax.ShapeDtypeStruct((main_rows, LANES), F32),
            jax.ShapeDtypeStruct((2 * na, LANES), F32),
            jax.ShapeDtypeStruct((2 * na, LANES), F32),
        ],
        scratch_shapes=[
            pltpu.VMEM((2, ext, 8, LANES), F32),
            pltpu.VMEM((2, ext, 8, LANES), F32),
            pltpu.VMEM((2, 2, ext, 16, LANES), F32),
            pltpu.VMEM((2, 2, ext, 16, LANES), F32),
            pltpu.VMEM((2, 2, ext, 16, LANES), F32),
            pltpu.VMEM((2, 2, ext, 16, LANES), F32),
            pltpu.VMEM((2, ext, 8, LANES), F32),
            pltpu.VMEM((2, ext, 8, LANES), F32),
            pltpu.VMEM((2, na, LANES, LANES), F32),
            pltpu.VMEM((16, LANES), F32),
        ],
    )(padded, prof, x)

    return pl.pallas_call(
        functools.partial(reduce_kernel, nb, na, n_chan, n_sub, harmonics, weight),
        in_specs=[whole] * 5,
        out_specs=[whole, whole, pl.BlockSpec(memory_space=pltpu.SMEM)],
        out_shape=[
            jax.ShapeDtypeStruct((2, owned), F32),
            jax.ShapeDtypeStruct((2, harmonics), F32),
            jax.ShapeDtypeStruct((1,), F32),
        ],
        scratch_shapes=[
            pltpu.VMEM((n_sub, main_rows, LANES), F32),
            pltpu.VMEM((n_sub, 2 * na, LANES), F32),
            pltpu.VMEM((n_sub, 2 * na, LANES), F32),
            pltpu.VMEM((n_chan, 2 * na + 8, LANES), F32),
            pltpu.VMEM((2 * na + 8, LANES), F32),
            dma((n_sub,)), dma((n_sub,)),
            dma((n_sub,)), dma((n_sub,)),
            dma((n_sub,)), dma((n_sub,)),
            dma((n_chan,)), dma((n_chan,)),
        ],
        compiler_params=pltpu.CompilerParams(collective_id=0, has_side_effects=True),
    )(filter_init, profile_init, main, tail, head)


def solution(mesh):
    return jax.shard_map(
        on_device,
        mesh=mesh,
        in_specs=(P("sub", None, None, "chan"), P(None, "chan"), P()),
        out_specs=(P(None, "chan"), P(), P()),
        check_vma=False,
    )
```

```python
import functools

import jax
import jax.numpy as jnp
from jax import lax
from jax.experimental import pallas as pl
from jax.experimental.pallas import tpu as pltpu
from jax.sharding import PartitionSpec as P

filter_rate = 0.1
profile_rate = 0.1
epsilon = 1e-06
LANES = 128
MESH = pl.DeviceIdType.MESH
F32 = jnp.float32


def lanes_of(shape):
    return lax.broadcasted_iota(jnp.int32, shape, len(shape) - 1)


def shift_right(x, k):
    rolled = pltpu.roll(x, k, 2)
    before = jnp.concatenate([rolled[-1:], rolled[:-1]], axis=0)
    return jnp.where(lanes_of(x.shape) >= k, rolled, before)


def shift_left(x, k):
    rolled = pltpu.roll(x, LANES - k, 2)
    after = jnp.concatenate([rolled[1:], rolled[:1]], axis=0)
    return jnp.where(lanes_of(x.shape) < LANES - k, rolled, after)


def by_sublane(x, shift):
    sub = lax.broadcasted_iota(jnp.int32, x.shape, 1)
    for k in (1, 2, 4):
        x = jnp.where((sub & k) != 0, shift(x, k), x)
    return x


def halo_kernel(nb, na, n_chan, f_ref, q_ref, pad_ref, prof_ref, low, high, s_sem, r_sem):
    chan = lax.axis_index("chan")
    sub = lax.axis_index("sub")
    above = lax.rem(chan + 1, n_chan)
    below = lax.rem(chan + n_chan - 1, n_chan)
    width = na * LANES
    owned = nb * LANES
    barrier = pltpu.get_barrier_semaphore()
    for c in (above, below):
        pl.semaphore_signal(barrier, inc=1, device_id=(c, sub), device_id_type=MESH)
    pl.semaphore_wait(barrier, 2)
    copies = [
        pltpu.make_async_remote_copy(
            src_ref=f_ref.at[:, pl.ds(start, width)], dst_ref=dst, send_sem=s_sem.at[i],
            recv_sem=r_sem.at[i], device_id=(c, sub), device_id_type=MESH,
        )
        for i, (start, dst, c) in enumerate(((owned - width, low, above), (0, high, below)))
    ]
    for copy in copies:
        copy.start()
    for ri in range(2):
        for n in range(nb):
            pad_ref[ri, na + n : na + n + 1] = f_ref[ri : ri + 1, n * LANES : (n + 1) * LANES]
        for a in range(na):
            row = q_ref[ri : ri + 1, a * LANES : (a + 1) * LANES]
            prof_ref[ri, a] = jnp.broadcast_to(row, (LANES, LANES)).T
    for copy in copies:
        copy.wait()
    has_low = chan > 0
    has_high = chan < n_chan - 1
    for ri in range(2):
        for n in range(na):
            cols = slice(n * LANES, (n + 1) * LANES)
            pad_ref[ri, n : n + 1] = jnp.where(has_low, low[ri : ri + 1, cols], 0.0)
            row = na + nb + n
            pad_ref[ri, row : row + 1] = jnp.where(has_high, high[ri : ri + 1, cols], 0.0)


def gradient_kernel(
    nb, na, factor, f_ref, q_ref, x_ref, main_ref, tail_ref, head_ref,
    base_f, base_b, fwd0, bwd0, up0, lo0, fwd1, bwd1, up1, lo1,
    up_all, lo_all, prof_acc, err_acc,
):
    pair = pl.program_id(0)
    last_pair = pl.num_programs(0) - 1
    last = 2 * pl.num_programs(0) - 1
    sets = ((fwd0, bwd0, up0, lo0), (fwd1, bwd1, up1, lo1))
    ext = nb + na
    tile = (8, LANES)
    pairs = [(ri, g) for ri in range(2) for g in range(2)]
    lane = lanes_of(tile)
    zero8 = jnp.zeros(tile, F32)

    def rows(g):
        return slice(8 * g, 8 * g + 8)

    def shifts(step):
        right = [lax.rem(16 * step + 8 * g, LANES) for g in range(2)]
        left = [lax.rem(LANES - t, LANES) for t in right]
        keep_right = [lane >= t for t in right]
        keep_left = [lane < LANES - t for t in right]
        return right, left, keep_right, keep_left

    def build_fwd(step, fwd):
        _, left, _, keep = shifts(step)
        init = tuple(pltpu.roll(base_f[ri, 0], left[g], 1) for ri, g in pairs)

        def one(n, carry):
            out = []
            for (ri, g), now in zip(pairs, carry):
                after = pltpu.roll(base_f[ri, n + 1], left[g], 1)
                fwd[ri, n, rows(g)] = jnp.where(keep[g], now, after)
                out.append(after)
            return tuple(out)

        return init, one, ext - 1

    def build_bwd(step, bwd):
        right, _, keep, _ = shifts(step)
        init = tuple(pltpu.roll(base_b[ri, 0], right[g], 1) for ri, g in pairs)

        def one(n, carry):
            out = []
            for (ri, g), before in zip(pairs, carry):
                now = pltpu.roll(base_b[ri, n + 1], right[g], 1)
                bwd[ri, n + 1, rows(g)] = jnp.where(keep[g], now, before)
                out.append(now)
            return tuple(out)

        return init, one, ext - 1

    def add_shifted(total, shift, pick):
        def run(step, parts):
            amount, keep = shift(step)
            init = (zero8,) * 4

            def one(n, carry):
                out = []
                sums = [total[ri, n] for ri in range(2)]
                for (ri, g), before in zip(pairs, carry):
                    now = pltpu.roll(parts[ri, n, rows(g)], amount[g], 1)
                    sums[ri] = sums[ri] + pick(keep[g], now, before)
                    out.append(now)
                for ri in range(2):
                    total[ri, n] = sums[ri]
                return tuple(out)

            return init, one, ext

        return run

    def right_of(step):
        right, _, keep, _ = shifts(step)
        return right, keep

    def left_of(step):
        _, left, _, keep = shifts(step)
        return left, keep

    shear_up = add_shifted(up_all, right_of, lambda k, now, before: jnp.where(k, now, before))
    shear_lo = add_shifted(lo_all, left_of, lambda k, now, before: jnp.where(k, before, now))

    def run_all(task):
        init, one, count = task
        for n in range(count):
            init = one(n, init)

    @pl.when(pair == 0)
    def _():
        for ri in range(2):
            high = jnp.broadcast_to(f_ref[ri, na:, :][:, None, :], (ext, 8, LANES))
            base_f[ri] = by_sublane(high, shift_left)
            low = jnp.broadcast_to(f_ref[ri, :ext, :][:, None, :], (ext, 8, LANES))
            base_b[ri] = by_sublane(low, shift_right)
        up_all[...] = jnp.zeros_like(up_all)
        lo_all[...] = jnp.zeros_like(lo_all)
        for _, _, up, lo in sets:
            up[...] = jnp.zeros_like(up)
            lo[...] = jnp.zeros_like(lo)
        err_acc[...] = jnp.zeros_like(err_acc)
        run_all(build_fwd(0 * pair, fwd0))
        run_all(build_bwd(0 * pair, bwd0))

    for half in range(2):
        m = 2 * pair + half
        held = slice(16 * half, 16 * half + 16)
        fwd, bwd, up, lo = sets[half]
        next_fwd, next_bwd, prev_up, prev_lo = sets[1 - half]
        for ri in range(2):
            for n in range(na - 1):
                up[ri, nb + n] = jnp.zeros((16, LANES), F32)
                lo[ri, n] = jnp.zeros((16, LANES), F32)

        tasks = [
            build_fwd(m + 1, next_fwd), build_bwd(m + 1, next_bwd),
            shear_up(m + last, prev_up), shear_lo(m + last, prev_lo),
        ]
        for a in range(na):
            qr = q_ref[0, a, held]
            qi = q_ref[1, a, held]
            init, side, count = tasks[a] if a < 4 else ((), lambda n, carry: carry, 0)

            def body(b, carry, a=a, qr=qr, qi=qi, side=side):
                gr, gi, er, beside = carry
                cols = pl.ds(pl.multiple_of(b * LANES, LANES), LANES)
                xr = x_ref[0, a, held, cols].astype(F32)
                xi = x_ref[1, a, held, cols].astype(F32)
                fr, fi = fwd[0, b + a], fwd[1, b + a]
                br, bi = bwd[0, b - a + na], bwd[1, b - a + na]
                beside = side(b, beside)
                pr = fr * br + fi * bi
                pi = fi * br - fr * bi
                rr = xr - (pr * qr - pi * qi)
                ri = xi - (pr * qi + pi * qr)
                er = er + (rr * rr + ri * ri)
                gr = gr + (rr * pr + ri * pi)
                gi = gi + (ri * pr - rr * pi)
                yr = rr * qr + ri * qi
                yi = ri * qr - rr * qi
                ur = yr * br - yi * bi
                ui = yr * bi + yi * br
                vr = yr * fr + yi * fi
                vi = yr * fi - yi * fr
                iu, il = b + a, b - a + na - 1
                if a == 0:
                    up[0, iu] = ur
                    up[1, iu] = ui
                    lo[0, il] = vr
                    lo[1, il] = vi
                else:
                    up[0, iu] = up[0, iu] + ur
                    up[1, iu] = up[1, iu] + ui
                    lo[0, il] = lo[0, il] + vr
                    lo[1, il] = lo[1, il] + vi
                return gr, gi, er, beside

            zero = jnp.zeros((16, LANES), F32)
            gr, gi, er, beside = lax.fori_loop(0, nb, body, (zero, zero, zero, init), unroll=4)
            for n in range(nb, count):
                beside = side(n, beside)
            group = pl.ds(pl.multiple_of(16 * m, 16), 16)
            prof_acc[0, a, group] = gr
            prof_acc[1, a, group] = gi
            err_acc[...] = err_acc[...] + er
        for task in tasks[na:]:
            run_all(task)

    @pl.when(pair == last_pair)
    def _():
        run_all(shear_up(2 * pair + 1, up1))
        run_all(shear_lo(2 * pair + 1, lo1))
        for ri in range(2):
            upper = factor * jnp.sum(by_sublane(up_all[ri], shift_right), axis=1)
            lower = factor * jnp.sum(by_sublane(lo_all[ri], shift_left), axis=1)
            main_ref[ri * nb : (ri + 1) * nb] = upper[:nb] + lower[na:]
            tail_ref[ri * na : (ri + 1) * na] = upper[nb:]
            head_ref[ri * na : (ri + 1) * na] = lower[:na]
            for a in range(na):
                sums = lax.dot_general(
                    jnp.ones(tile, F32), prof_acc[ri, a], (((1,), (1,)), ((), ())),
                    precision=lax.Precision.HIGHEST, preferred_element_type=F32,
                )
                row = 2 * nb + ri * na + a
                main_ref[row : row + 1] = factor * sums[:1]
        main_ref[2 * nb + 2 * na : 2 * nb + 2 * na + 1] = jnp.sum(
            err_acc[...], axis=0, keepdims=True
        )


def reduce_kernel(
    nb, na, n_chan, n_sub, harmonics, weight, main_ref, tail_ref, head_ref,
    out_ref, prof_ref, misfit_ref,
    mains, tails, heads, packs, pack,
    s_main, r_main, s_tail, r_tail, s_head, r_head, s_pack, r_pack,
):
    chan = lax.axis_index("chan")
    sub = lax.axis_index("sub")
    above = lax.rem(chan + 1, n_chan)
    below = lax.rem(chan + n_chan - 1, n_chan)

    barrier = pltpu.get_barrier_semaphore()
    greeted = 0
    for off in range(n_sub):
        peer = lax.rem(sub + off, n_sub)
        for c in (above, below) + ((chan,) if off else ()):
            pl.semaphore_signal(barrier, inc=1, device_id=(c, peer), device_id_type=MESH)
            greeted += 1
    for off in range(2, n_chan - 1):
        pl.semaphore_signal(
            barrier, inc=1, device_id=(lax.rem(chan + off, n_chan), sub), device_id_type=MESH
        )
        greeted += 1
    pl.semaphore_wait(barrier, greeted)

    def copy_to(src, dst, send, recv, device):
        return pltpu.make_async_remote_copy(
            src_ref=src, dst_ref=dst, send_sem=send, recv_sem=recv,
            device_id=device, device_id_type=MESH,
        )

    sends = []
    for off in range(1, n_sub):
        peer = lax.rem(sub + off, n_sub)
        sends.append(
            copy_to(main_ref, mains.at[sub], s_main.at[off], r_main.at[sub], (chan, peer))
        )
    for off in range(n_sub):
        peer = lax.rem(sub + off, n_sub)
        sends.append(
            copy_to(tail_ref, tails.at[sub], s_tail.at[off], r_tail.at[sub], (above, peer))
        )
        sends.append(
            copy_to(head_ref, heads.at[sub], s_head.at[off], r_head.at[sub], (below, peer))
        )
    for copy in sends:
        copy.start()
    mains[sub] = main_ref[...]
    for off in range(n_sub):
        peer = lax.rem(sub + off, n_sub)
        if off:
            copy_to(
                main_ref, mains.at[peer], s_main.at[off], r_main.at[peer], (chan, peer)
            ).wait_recv()
        copy_to(
            tail_ref, tails.at[peer], s_tail.at[off], r_tail.at[peer], (above, peer)
        ).wait_recv()
        copy_to(
            head_ref, heads.at[peer], s_head.at[off], r_head.at[peer], (below, peer)
        ).wait_recv()

    total = mains[0]
    tail = tails[0]
    head = heads[0]
    for s in range(1, n_sub):
        total = total + mains[s]
        tail = tail + tails[s]
        head = head + heads[s]
    tail = jnp.where(chan > 0, tail, 0.0)
    head = jnp.where(chan < n_chan - 1, head, 0.0)
    grads = []
    squares = jnp.zeros((1, LANES), F32)
    for ri in range(2):
        own = total[ri * nb : (ri + 1) * nb]
        part = slice(ri * na, (ri + 1) * na)
        grad = jnp.concatenate([own[:na] + tail[part], own[na:]], axis=0)
        grad = jnp.concatenate([grad[: nb - na], grad[nb - na :] + head[part]], axis=0)
        squares = squares + jnp.sum(grad * grad, axis=0, keepdims=True)
        grads.append(grad)
    prof_rows = 2 * na
    pack[...] = jnp.zeros_like(pack)
    pack[: prof_rows + 1] = total[2 * nb : 2 * nb + prof_rows + 1]
    pack[prof_rows + 1 : prof_rows + 2] = squares
    packs[chan] = pack[...]

    for copy in sends:
        copy.wait_send()
    exchanges = []
    for off in range(1, n_chan):
        peer = lax.rem(chan + off, n_chan)
        exchanges.append(
            copy_to(pack, packs.at[chan], s_pack.at[off], r_pack.at[chan], (peer, sub))
        )
    for copy in exchanges:
        copy.start()
    for off in range(1, n_chan):
        peer = lax.rem(chan + off, n_chan)
        copy_to(pack, packs.at[peer], s_pack.at[off], r_pack.at[peer], (peer, sub)).wait_recv()
    sums = packs[0]
    for c in range(1, n_chan):
        sums = sums + packs[c]
    prof_grad = sums[:prof_rows]
    error = jnp.sum(sums[prof_rows : prof_rows + 1])
    square = jnp.sum(sums[prof_rows + 1 : prof_rows + 2], axis=1, keepdims=True)
    channels = n_chan * nb * LANES
    misfit_ref[0] = error * (weight / channels)
    scale = filter_rate / jnp.sqrt(square / (2 * channels) + epsilon)
    for ri in range(2):
        step = grads[ri] * scale
        for n in range(nb):
            cols = slice(n * LANES, (n + 1) * LANES)
            out_ref[ri : ri + 1, cols] = step[n : n + 1]
    mean = jnp.sum(prof_grad * prof_grad, keepdims=True) / (2 * harmonics)
    prof_step = prof_grad * (profile_rate / jnp.sqrt(mean + epsilon))
    for ri in range(2):
        for a in range(na):
            cols = slice(a * LANES, (a + 1) * LANES)
            row = ri * na + a
            prof_ref[ri : ri + 1, cols] = prof_step[row : row + 1]
    for copy in exchanges:
        copy.wait_send()


def on_device(spectra, filter_init, profile_init):
    harmonics = profile_init.shape[1]
    owned = filter_init.shape[1]
    n_chan = lax.axis_size("chan")
    n_sub = lax.axis_size("sub")
    nb = owned // LANES
    na = harmonics // LANES
    ext = nb + na
    weight = 1.0 / (n_sub * spectra.shape[0] * harmonics)
    factor = -2.0 * weight
    main_rows = 2 * nb + 2 * na + 8

    whole = pl.BlockSpec(memory_space=pltpu.VMEM)
    dma = pltpu.SemaphoreType.DMA
    padded, prof = pl.pallas_call(
        functools.partial(halo_kernel, nb, na, n_chan),
        in_specs=[whole] * 2,
        out_specs=[whole] * 2,
        out_shape=[
            jax.ShapeDtypeStruct((2, nb + 2 * na, LANES), F32),
            jax.ShapeDtypeStruct((2, na, LANES, LANES), F32),
        ],
        scratch_shapes=[
            pltpu.VMEM((2, harmonics), F32), pltpu.VMEM((2, harmonics), F32), dma((2,)), dma((2,)),
        ],
        compiler_params=pltpu.CompilerParams(collective_id=1, has_side_effects=True),
    )(filter_init, profile_init)
    x = spectra.reshape(2, na, LANES, owned)

    main, tail, head = pl.pallas_call(
        functools.partial(gradient_kernel, nb, na, factor),
        grid=(LANES // 32,),
        in_specs=[
            pl.BlockSpec((2, nb + 2 * na, LANES), lambda m: (0, 0, 0)),
            pl.BlockSpec((2, na, 32, LANES), lambda m: (0, 0, m, 0)),
            pl.BlockSpec((2, na, 32, owned), lambda m: (0, 0, m, 0)),
        ],
        out_specs=[
            pl.BlockSpec((main_rows, LANES), lambda m: (0, 0)),
            pl.BlockSpec((2 * na, LANES), lambda m: (0, 0)),
            pl.BlockSpec((2 * na, LANES), lambda m: (0, 0)),
        ],
        out_shape=[
            jax.ShapeDtypeStruct((main_rows, LANES), F32),
            jax.ShapeDtypeStruct((2 * na, LANES), F32),
            jax.ShapeDtypeStruct((2 * na, LANES), F32),
        ],
        scratch_shapes=[
            pltpu.VMEM((2, ext, 8, LANES), F32),
            pltpu.VMEM((2, ext, 8, LANES), F32),
            pltpu.VMEM((2, ext, 16, LANES), F32),
            pltpu.VMEM((2, ext, 16, LANES), F32),
            pltpu.VMEM((2, ext, 16, LANES), F32),
            pltpu.VMEM((2, ext, 16, LANES), F32),
            pltpu.VMEM((2, ext, 16, LANES), F32),
            pltpu.VMEM((2, ext, 16, LANES), F32),
            pltpu.VMEM((2, ext, 16, LANES), F32),
            pltpu.VMEM((2, ext, 16, LANES), F32),
            pltpu.VMEM((2, ext, 8, LANES), F32),
            pltpu.VMEM((2, ext, 8, LANES), F32),
            pltpu.VMEM((2, na, LANES, LANES), F32),
            pltpu.VMEM((16, LANES), F32),
        ],
    )(padded, prof, x)

    step, prof_step, misfit = pl.pallas_call(
        functools.partial(reduce_kernel, nb, na, n_chan, n_sub, harmonics, weight),
        in_specs=[whole] * 3,
        out_specs=[whole, whole, pl.BlockSpec(memory_space=pltpu.SMEM)],
        out_shape=[
            jax.ShapeDtypeStruct((2, owned), F32),
            jax.ShapeDtypeStruct((2, harmonics), F32),
            jax.ShapeDtypeStruct((1,), F32),
        ],
        scratch_shapes=[
            pltpu.VMEM((n_sub, main_rows, LANES), F32),
            pltpu.VMEM((n_sub, 2 * na, LANES), F32),
            pltpu.VMEM((n_sub, 2 * na, LANES), F32),
            pltpu.VMEM((n_chan, 2 * na + 8, LANES), F32),
            pltpu.VMEM((2 * na + 8, LANES), F32),
            dma((n_sub,)), dma((n_sub,)),
            dma((n_sub,)), dma((n_sub,)),
            dma((n_sub,)), dma((n_sub,)),
            dma((n_chan,)), dma((n_chan,)),
        ],
        compiler_params=pltpu.CompilerParams(collective_id=0, has_side_effects=True),
    )(main, tail, head)
    return (filter_init - step, profile_init - prof_step, misfit)


def solution(mesh):
    return jax.shard_map(
        on_device,
        mesh=mesh,
        in_specs=(P("sub", None, None, "chan"), P(None, "chan"), P()),
        out_specs=(P(None, "chan"), P(), P()),
        check_vma=False,
    )
```

```python
import functools

import jax
import jax.numpy as jnp
from jax import lax
from jax.experimental import pallas as pl
from jax.experimental.pallas import tpu as pltpu
from jax.sharding import PartitionSpec as P

filter_rate = 0.1
profile_rate = 0.1
epsilon = 1e-06
LANES = 128
MESH = pl.DeviceIdType.MESH
F32 = jnp.float32


def lanes_of(shape):
    return lax.broadcasted_iota(jnp.int32, shape, len(shape) - 1)


def shift_right(x, k):
    rolled = pltpu.roll(x, k, 2)
    before = jnp.concatenate([rolled[-1:], rolled[:-1]], axis=0)
    return jnp.where(lanes_of(x.shape) >= k, rolled, before)


def shift_left(x, k):
    rolled = pltpu.roll(x, LANES - k, 2)
    after = jnp.concatenate([rolled[1:], rolled[:1]], axis=0)
    return jnp.where(lanes_of(x.shape) < LANES - k, rolled, after)


def by_sublane(x, shift):
    sub = lax.broadcasted_iota(jnp.int32, x.shape, 1)
    for k in (1, 2, 4):
        x = jnp.where((sub & k) != 0, shift(x, k), x)
    return x


def halo_kernel(nb, na, n_chan, f_ref, q_ref, pad_ref, prof_ref, low, high, s_sem, r_sem):
    chan = lax.axis_index("chan")
    sub = lax.axis_index("sub")
    above = lax.rem(chan + 1, n_chan)
    below = lax.rem(chan + n_chan - 1, n_chan)
    width = na * LANES
    owned = nb * LANES
    barrier = pltpu.get_barrier_semaphore()
    for c in (above, below):
        pl.semaphore_signal(barrier, inc=1, device_id=(c, sub), device_id_type=MESH)
    pl.semaphore_wait(barrier, 2)
    copies = [
        pltpu.make_async_remote_copy(
            src_ref=f_ref.at[:, pl.ds(start, width)], dst_ref=dst, send_sem=s_sem.at[i],
            recv_sem=r_sem.at[i], device_id=(c, sub), device_id_type=MESH,
        )
        for i, (start, dst, c) in enumerate(((owned - width, low, above), (0, high, below)))
    ]
    for copy in copies:
        copy.start()
    for ri in range(2):
        for n in range(nb):
            pad_ref[ri, na + n : na + n + 1] = f_ref[ri : ri + 1, n * LANES : (n + 1) * LANES]
        for a in range(na):
            row = q_ref[ri : ri + 1, a * LANES : (a + 1) * LANES]
            prof_ref[ri, a] = jnp.broadcast_to(row, (LANES, LANES)).T
    for copy in copies:
        copy.wait()
    has_low = chan > 0
    has_high = chan < n_chan - 1
    for ri in range(2):
        for n in range(na):
            cols = slice(n * LANES, (n + 1) * LANES)
            pad_ref[ri, n : n + 1] = jnp.where(has_low, low[ri : ri + 1, cols], 0.0)
            row = na + nb + n
            pad_ref[ri, row : row + 1] = jnp.where(has_high, high[ri : ri + 1, cols], 0.0)


def gradient_kernel(
    nb, na, factor, f_ref, q_ref, x_ref, main_ref, tail_ref, head_ref,
    base_f, base_b, fwd0, bwd0, up0, lo0, fwd1, bwd1, up1, lo1,
    up_all, lo_all, prof_acc, err_acc,
):
    pair = pl.program_id(0)
    last_pair = pl.num_programs(0) - 1
    last = 2 * pl.num_programs(0) - 1
    sets = ((fwd0, bwd0, up0, lo0), (fwd1, bwd1, up1, lo1))
    ext = nb + na
    tile = (8, LANES)
    pairs = [(ri, g) for ri in range(2) for g in range(2)]
    lane = lanes_of(tile)
    zero8 = jnp.zeros(tile, F32)

    def rows(g):
        return slice(8 * g, 8 * g + 8)

    def shifts(step):
        right = [lax.rem(16 * step + 8 * g, LANES) for g in range(2)]
        left = [lax.rem(LANES - t, LANES) for t in right]
        keep_right = [lane >= t for t in right]
        keep_left = [lane < LANES - t for t in right]
        return right, left, keep_right, keep_left

    def build_fwd(step, fwd):
        _, left, _, keep = shifts(step)
        init = tuple(pltpu.roll(base_f[ri, 0], left[g], 1) for ri, g in pairs)

        def one(n, carry):
            out = []
            for (ri, g), now in zip(pairs, carry):
                after = pltpu.roll(base_f[ri, n + 1], left[g], 1)
                fwd[ri, n, rows(g)] = jnp.where(keep[g], now, after)
                out.append(after)
            return tuple(out)

        return init, one, ext - 1

    def build_bwd(step, bwd):
        right, _, keep, _ = shifts(step)
        init = tuple(pltpu.roll(base_b[ri, 0], right[g], 1) for ri, g in pairs)

        def one(n, carry):
            out = []
            for (ri, g), before in zip(pairs, carry):
                now = pltpu.roll(base_b[ri, n + 1], right[g], 1)
                bwd[ri, n + 1, rows(g)] = jnp.where(keep[g], now, before)
                out.append(now)
            return tuple(out)

        return init, one, ext - 1

    def add_shifted(total, shift, pick):
        def run(step, parts):
            amount, keep = shift(step)
            init = (zero8,) * 4

            def one(n, carry):
                out = []
                sums = [total[ri, n] for ri in range(2)]
                for (ri, g), before in zip(pairs, carry):
                    now = pltpu.roll(parts[ri, n, rows(g)], amount[g], 1)
                    sums[ri] = sums[ri] + pick(keep[g], now, before)
                    out.append(now)
                for ri in range(2):
                    total[ri, n] = sums[ri]
                return tuple(out)

            return init, one, ext

        return run

    def right_of(step):
        right, _, keep, _ = shifts(step)
        return right, keep

    def left_of(step):
        _, left, _, keep = shifts(step)
        return left, keep

    shear_up = add_shifted(up_all, right_of, lambda k, now, before: jnp.where(k, now, before))
    shear_lo = add_shifted(lo_all, left_of, lambda k, now, before: jnp.where(k, before, now))

    def run_all(task):
        init, one, count = task
        for n in range(count):
            init = one(n, init)

    @pl.when(pair == 0)
    def _():
        for ri in range(2):
            high = jnp.broadcast_to(f_ref[ri, na:, :][:, None, :], (ext, 8, LANES))
            base_f[ri] = by_sublane(high, shift_left)
            low = jnp.broadcast_to(f_ref[ri, :ext, :][:, None, :], (ext, 8, LANES))
            base_b[ri] = by_sublane(low, shift_right)
        up_all[...] = jnp.zeros_like(up_all)
        lo_all[...] = jnp.zeros_like(lo_all)
        for _, _, up, lo in sets:
            up[...] = jnp.zeros_like(up)
            lo[...] = jnp.zeros_like(lo)
        err_acc[...] = jnp.zeros_like(err_acc)
        run_all(build_fwd(0 * pair, fwd0))
        run_all(build_bwd(0 * pair, bwd0))

    for half in range(2):
        m = 2 * pair + half
        held = slice(16 * half, 16 * half + 16)
        fwd, bwd, up, lo = sets[half]
        next_fwd, next_bwd, prev_up, prev_lo = sets[1 - half]
        for ri in range(2):
            for n in range(na - 1):
                up[ri, nb + n] = jnp.zeros((16, LANES), F32)
                lo[ri, n] = jnp.zeros((16, LANES), F32)

        tasks = [
            build_fwd(m + 1, next_fwd), build_bwd(m + 1, next_bwd),
            shear_up(m + last, prev_up), shear_lo(m + last, prev_lo),
        ]
        for a in range(na):
            qr = q_ref[0, a, held]
            qi = q_ref[1, a, held]
            init, side, count = tasks[a] if a < 4 else ((), lambda n, carry: carry, 0)

            def body(b, carry, a=a, qr=qr, qi=qi, side=side):
                gr, gi, er, beside = carry
                cols = pl.ds(pl.multiple_of(b * LANES, LANES), LANES)
                xr = x_ref[0, a, held, cols].astype(F32)
                xi = x_ref[1, a, held, cols].astype(F32)
                fr, fi = fwd[0, b + a], fwd[1, b + a]
                br, bi = bwd[0, b - a + na], bwd[1, b - a + na]
                beside = side(b, beside)
                pr = fr * br + fi * bi
                pi = fi * br - fr * bi
                rr = xr - (pr * qr - pi * qi)
                ri = xi - (pr * qi + pi * qr)
                er = er + (rr * rr + ri * ri)
                gr = gr + (rr * pr + ri * pi)
                gi = gi + (ri * pr - rr * pi)
                yr = rr * qr + ri * qi
                yi = ri * qr - rr * qi
                ur = yr * br - yi * bi
                ui = yr * bi + yi * br
                vr = yr * fr + yi * fi
                vi = yr * fi - yi * fr
                iu, il = b + a, b - a + na - 1
                if a == 0:
                    up[0, iu] = ur
                    up[1, iu] = ui
                    lo[0, il] = vr
                    lo[1, il] = vi
                else:
                    up[0, iu] = up[0, iu] + ur
                    up[1, iu] = up[1, iu] + ui
                    lo[0, il] = lo[0, il] + vr
                    lo[1, il] = lo[1, il] + vi
                return gr, gi, er, beside

            zero = jnp.zeros((16, LANES), F32)
            gr, gi, er, beside = lax.fori_loop(0, nb, body, (zero, zero, zero, init), unroll=nb)
            for n in range(nb, count):
                beside = side(n, beside)
            group = pl.ds(pl.multiple_of(16 * m, 16), 16)
            prof_acc[0, a, group] = gr
            prof_acc[1, a, group] = gi
            err_acc[...] = err_acc[...] + er
        for task in tasks[na:]:
            run_all(task)

    @pl.when(pair == last_pair)
    def _():
        run_all(shear_up(2 * pair + 1, up1))
        run_all(shear_lo(2 * pair + 1, lo1))
        for ri in range(2):
            upper = factor * jnp.sum(by_sublane(up_all[ri], shift_right), axis=1)
            lower = factor * jnp.sum(by_sublane(lo_all[ri], shift_left), axis=1)
            main_ref[ri * nb : (ri + 1) * nb] = upper[:nb] + lower[na:]
            tail_ref[ri * na : (ri + 1) * na] = upper[nb:]
            head_ref[ri * na : (ri + 1) * na] = lower[:na]
            for a in range(na):
                sums = lax.dot_general(
                    jnp.ones(tile, F32), prof_acc[ri, a], (((1,), (1,)), ((), ())),
                    precision=lax.Precision.HIGHEST, preferred_element_type=F32,
                )
                row = 2 * nb + ri * na + a
                main_ref[row : row + 1] = factor * sums[:1]
        main_ref[2 * nb + 2 * na : 2 * nb + 2 * na + 1] = jnp.sum(
            err_acc[...], axis=0, keepdims=True
        )


def reduce_kernel(
    nb, na, n_chan, n_sub, harmonics, weight, main_ref, tail_ref, head_ref,
    out_ref, prof_ref, misfit_ref,
    mains, tails, heads, packs, pack,
    s_main, r_main, s_tail, r_tail, s_head, r_head, s_pack, r_pack,
):
    chan = lax.axis_index("chan")
    sub = lax.axis_index("sub")
    above = lax.rem(chan + 1, n_chan)
    below = lax.rem(chan + n_chan - 1, n_chan)

    barrier = pltpu.get_barrier_semaphore()
    greeted = 0
    for off in range(n_sub):
        peer = lax.rem(sub + off, n_sub)
        for c in (above, below) + ((chan,) if off else ()):
            pl.semaphore_signal(barrier, inc=1, device_id=(c, peer), device_id_type=MESH)
            greeted += 1
    for off in range(2, n_chan - 1):
        pl.semaphore_signal(
            barrier, inc=1, device_id=(lax.rem(chan + off, n_chan), sub), device_id_type=MESH
        )
        greeted += 1
    pl.semaphore_wait(barrier, greeted)

    def copy_to(src, dst, send, recv, device):
        return pltpu.make_async_remote_copy(
            src_ref=src, dst_ref=dst, send_sem=send, recv_sem=recv,
            device_id=device, device_id_type=MESH,
        )

    sends = []
    for off in range(1, n_sub):
        peer = lax.rem(sub + off, n_sub)
        sends.append(
            copy_to(main_ref, mains.at[sub], s_main.at[off], r_main.at[sub], (chan, peer))
        )
    for off in range(n_sub):
        peer = lax.rem(sub + off, n_sub)
        sends.append(
            copy_to(tail_ref, tails.at[sub], s_tail.at[off], r_tail.at[sub], (above, peer))
        )
        sends.append(
            copy_to(head_ref, heads.at[sub], s_head.at[off], r_head.at[sub], (below, peer))
        )
    for copy in sends:
        copy.start()
    mains[sub] = main_ref[...]
    for off in range(n_sub):
        peer = lax.rem(sub + off, n_sub)
        if off:
            copy_to(
                main_ref, mains.at[peer], s_main.at[off], r_main.at[peer], (chan, peer)
            ).wait_recv()
        copy_to(
            tail_ref, tails.at[peer], s_tail.at[off], r_tail.at[peer], (above, peer)
        ).wait_recv()
        copy_to(
            head_ref, heads.at[peer], s_head.at[off], r_head.at[peer], (below, peer)
        ).wait_recv()

    total = mains[0]
    tail = tails[0]
    head = heads[0]
    for s in range(1, n_sub):
        total = total + mains[s]
        tail = tail + tails[s]
        head = head + heads[s]
    tail = jnp.where(chan > 0, tail, 0.0)
    head = jnp.where(chan < n_chan - 1, head, 0.0)
    grads = []
    squares = jnp.zeros((1, LANES), F32)
    for ri in range(2):
        own = total[ri * nb : (ri + 1) * nb]
        part = slice(ri * na, (ri + 1) * na)
        grad = jnp.concatenate([own[:na] + tail[part], own[na:]], axis=0)
        grad = jnp.concatenate([grad[: nb - na], grad[nb - na :] + head[part]], axis=0)
        squares = squares + jnp.sum(grad * grad, axis=0, keepdims=True)
        grads.append(grad)
    prof_rows = 2 * na
    pack[...] = jnp.zeros_like(pack)
    pack[: prof_rows + 1] = total[2 * nb : 2 * nb + prof_rows + 1]
    pack[prof_rows + 1 : prof_rows + 2] = squares
    packs[chan] = pack[...]

    for copy in sends:
        copy.wait_send()
    exchanges = []
    for off in range(1, n_chan):
        peer = lax.rem(chan + off, n_chan)
        exchanges.append(
            copy_to(pack, packs.at[chan], s_pack.at[off], r_pack.at[chan], (peer, sub))
        )
    for copy in exchanges:
        copy.start()
    for off in range(1, n_chan):
        peer = lax.rem(chan + off, n_chan)
        copy_to(pack, packs.at[peer], s_pack.at[off], r_pack.at[peer], (peer, sub)).wait_recv()
    sums = packs[0]
    for c in range(1, n_chan):
        sums = sums + packs[c]
    prof_grad = sums[:prof_rows]
    error = jnp.sum(sums[prof_rows : prof_rows + 1])
    square = jnp.sum(sums[prof_rows + 1 : prof_rows + 2], axis=1, keepdims=True)
    channels = n_chan * nb * LANES
    misfit_ref[0] = error * (weight / channels)
    scale = filter_rate / jnp.sqrt(square / (2 * channels) + epsilon)
    for ri in range(2):
        step = grads[ri] * scale
        for n in range(nb):
            cols = slice(n * LANES, (n + 1) * LANES)
            out_ref[ri : ri + 1, cols] = step[n : n + 1]
    mean = jnp.sum(prof_grad * prof_grad, keepdims=True) / (2 * harmonics)
    prof_step = prof_grad * (profile_rate / jnp.sqrt(mean + epsilon))
    for ri in range(2):
        for a in range(na):
            cols = slice(a * LANES, (a + 1) * LANES)
            row = ri * na + a
            prof_ref[ri : ri + 1, cols] = prof_step[row : row + 1]
    for copy in exchanges:
        copy.wait_send()


def on_device(spectra, filter_init, profile_init):
    harmonics = profile_init.shape[1]
    owned = filter_init.shape[1]
    n_chan = lax.axis_size("chan")
    n_sub = lax.axis_size("sub")
    nb = owned // LANES
    na = harmonics // LANES
    ext = nb + na
    weight = 1.0 / (n_sub * spectra.shape[0] * harmonics)
    factor = -2.0 * weight
    main_rows = 2 * nb + 2 * na + 8

    whole = pl.BlockSpec(memory_space=pltpu.VMEM)
    dma = pltpu.SemaphoreType.DMA
    padded, prof = pl.pallas_call(
        functools.partial(halo_kernel, nb, na, n_chan),
        in_specs=[whole] * 2,
        out_specs=[whole] * 2,
        out_shape=[
            jax.ShapeDtypeStruct((2, nb + 2 * na, LANES), F32),
            jax.ShapeDtypeStruct((2, na, LANES, LANES), F32),
        ],
        scratch_shapes=[
            pltpu.VMEM((2, harmonics), F32), pltpu.VMEM((2, harmonics), F32), dma((2,)), dma((2,)),
        ],
        compiler_params=pltpu.CompilerParams(collective_id=1, has_side_effects=True),
    )(filter_init, profile_init)
    x = spectra.reshape(2, na, LANES, owned)

    main, tail, head = pl.pallas_call(
        functools.partial(gradient_kernel, nb, na, factor),
        grid=(LANES // 32,),
        in_specs=[
            pl.BlockSpec((2, nb + 2 * na, LANES), lambda m: (0, 0, 0)),
            pl.BlockSpec((2, na, 32, LANES), lambda m: (0, 0, m, 0)),
            pl.BlockSpec((2, na, 32, owned), lambda m: (0, 0, m, 0)),
        ],
        out_specs=[
            pl.BlockSpec((main_rows, LANES), lambda m: (0, 0)),
            pl.BlockSpec((2 * na, LANES), lambda m: (0, 0)),
            pl.BlockSpec((2 * na, LANES), lambda m: (0, 0)),
        ],
        out_shape=[
            jax.ShapeDtypeStruct((main_rows, LANES), F32),
            jax.ShapeDtypeStruct((2 * na, LANES), F32),
            jax.ShapeDtypeStruct((2 * na, LANES), F32),
        ],
        scratch_shapes=[
            pltpu.VMEM((2, ext, 8, LANES), F32),
            pltpu.VMEM((2, ext, 8, LANES), F32),
            pltpu.VMEM((2, ext, 16, LANES), F32),
            pltpu.VMEM((2, ext, 16, LANES), F32),
            pltpu.VMEM((2, ext, 16, LANES), F32),
            pltpu.VMEM((2, ext, 16, LANES), F32),
            pltpu.VMEM((2, ext, 16, LANES), F32),
            pltpu.VMEM((2, ext, 16, LANES), F32),
            pltpu.VMEM((2, ext, 16, LANES), F32),
            pltpu.VMEM((2, ext, 16, LANES), F32),
            pltpu.VMEM((2, ext, 8, LANES), F32),
            pltpu.VMEM((2, ext, 8, LANES), F32),
            pltpu.VMEM((2, na, LANES, LANES), F32),
            pltpu.VMEM((16, LANES), F32),
        ],
    )(padded, prof, x)

    step, prof_step, misfit = pl.pallas_call(
        functools.partial(reduce_kernel, nb, na, n_chan, n_sub, harmonics, weight),
        in_specs=[whole] * 3,
        out_specs=[whole, whole, pl.BlockSpec(memory_space=pltpu.SMEM)],
        out_shape=[
            jax.ShapeDtypeStruct((2, owned), F32),
            jax.ShapeDtypeStruct((2, harmonics), F32),
            jax.ShapeDtypeStruct((1,), F32),
        ],
        scratch_shapes=[
            pltpu.VMEM((n_sub, main_rows, LANES), F32),
            pltpu.VMEM((n_sub, 2 * na, LANES), F32),
            pltpu.VMEM((n_sub, 2 * na, LANES), F32),
            pltpu.VMEM((n_chan, 2 * na + 8, LANES), F32),
            pltpu.VMEM((2 * na + 8, LANES), F32),
            dma((n_sub,)), dma((n_sub,)),
            dma((n_sub,)), dma((n_sub,)),
            dma((n_sub,)), dma((n_sub,)),
            dma((n_chan,)), dma((n_chan,)),
        ],
        compiler_params=pltpu.CompilerParams(collective_id=0, has_side_effects=True),
    )(main, tail, head)
    return (filter_init - step, profile_init - prof_step, misfit)


def solution(mesh):
    return jax.shard_map(
        on_device,
        mesh=mesh,
        in_specs=(P("sub", None, None, "chan"), P(None, "chan"), P()),
        out_specs=(P(None, "chan"), P(), P()),
        check_vma=False,
    )
```

```python
import functools

import jax
import jax.numpy as jnp
from jax import lax
from jax.experimental import pallas as pl
from jax.experimental.pallas import tpu as pltpu
from jax.sharding import PartitionSpec as P

filter_rate = 0.1
profile_rate = 0.1
epsilon = 1e-06
LANES = 128
MESH = pl.DeviceIdType.MESH
F32 = jnp.float32


def lanes_of(shape):
    return lax.broadcasted_iota(jnp.int32, shape, len(shape) - 1)


def shift_right(x, k):
    rolled = pltpu.roll(x, k, 2)
    before = jnp.concatenate([rolled[-1:], rolled[:-1]], axis=0)
    return jnp.where(lanes_of(x.shape) >= k, rolled, before)


def shift_left(x, k):
    rolled = pltpu.roll(x, LANES - k, 2)
    after = jnp.concatenate([rolled[1:], rolled[:1]], axis=0)
    return jnp.where(lanes_of(x.shape) < LANES - k, rolled, after)


def by_sublane(x, shift):
    sub = lax.broadcasted_iota(jnp.int32, x.shape, 1)
    for k in (1, 2, 4):
        x = jnp.where((sub & k) != 0, shift(x, k), x)
    return x


def halo_part(nb, na, n_chan, n_sub, f_ref, q_ref, pad_ref, prof_ref, low, high, s_sem, r_sem):
    chan = lax.axis_index("chan")
    sub = lax.axis_index("sub")
    above = lax.rem(chan + 1, n_chan)
    below = lax.rem(chan + n_chan - 1, n_chan)
    width = na * LANES
    owned = nb * LANES
    barrier = pltpu.get_barrier_semaphore()
    greeted = 0
    for off in range(n_sub):
        peer = lax.rem(sub + off, n_sub)
        for c in (above, below) + ((chan,) if off else ()):
            pl.semaphore_signal(barrier, inc=1, device_id=(c, peer), device_id_type=MESH)
            greeted += 1
    for off in range(2, n_chan - 1):
        pl.semaphore_signal(
            barrier, inc=1, device_id=(lax.rem(chan + off, n_chan), sub), device_id_type=MESH
        )
        greeted += 1
    for ri in range(2):
        for n in range(nb):
            pad_ref[ri, na + n : na + n + 1] = f_ref[ri : ri + 1, n * LANES : (n + 1) * LANES]
        for a in range(na):
            row = q_ref[ri : ri + 1, a * LANES : (a + 1) * LANES]
            prof_ref[ri, a] = jnp.broadcast_to(row, (LANES, LANES)).T
    pl.semaphore_wait(barrier, greeted)
    copies = [
        pltpu.make_async_remote_copy(
            src_ref=f_ref.at[:, pl.ds(start, width)], dst_ref=dst, send_sem=s_sem.at[i],
            recv_sem=r_sem.at[i], device_id=(c, sub), device_id_type=MESH,
        )
        for i, (start, dst, c) in enumerate(((owned - width, low, above), (0, high, below)))
    ]
    for copy in copies:
        copy.start()
    for copy in copies:
        copy.wait()
    has_low = chan > 0
    has_high = chan < n_chan - 1
    for ri in range(2):
        for n in range(na):
            cols = slice(n * LANES, (n + 1) * LANES)
            pad_ref[ri, n : n + 1] = jnp.where(has_low, low[ri : ri + 1, cols], 0.0)
            row = na + nb + n
            pad_ref[ri, row : row + 1] = jnp.where(has_high, high[ri : ri + 1, cols], 0.0)


def gradient_kernel(
    nb, na, n_chan, n_sub, harmonics, weight, factor, filter_ref, profile_ref, x_ref,
    out_ref, prof_ref, misfit_ref,
    f_ref, q_ref, halo_low, halo_high, s_halo, r_halo, main_ref, tail_ref, head_ref, reduce_refs,
    base_f, base_b, fwd0, bwd0, up0, lo0, fwd1, bwd1, up1, lo1,
    up_all, lo_all, prof_acc, err_acc,
):
    pair = pl.program_id(0)
    last_pair = pl.num_programs(0) - 1
    last = 2 * pl.num_programs(0) - 1
    sets = ((fwd0, bwd0, up0, lo0), (fwd1, bwd1, up1, lo1))
    ext = nb + na
    tile = (8, LANES)
    pairs = [(ri, g) for ri in range(2) for g in range(2)]
    lane = lanes_of(tile)
    zero8 = jnp.zeros(tile, F32)

    def rows(g):
        return slice(8 * g, 8 * g + 8)

    def shifts(step):
        right = [lax.rem(16 * step + 8 * g, LANES) for g in range(2)]
        left = [lax.rem(LANES - t, LANES) for t in right]
        keep_right = [lane >= t for t in right]
        keep_left = [lane < LANES - t for t in right]
        return right, left, keep_right, keep_left

    def build_fwd(step, fwd):
        _, left, _, keep = shifts(step)
        init = tuple(pltpu.roll(base_f[ri, 0], left[g], 1) for ri, g in pairs)

        def one(n, carry):
            out = []
            for (ri, g), now in zip(pairs, carry):
                after = pltpu.roll(base_f[ri, n + 1], left[g], 1)
                fwd[ri, n, rows(g)] = jnp.where(keep[g], now, after)
                out.append(after)
            return tuple(out)

        return init, one, ext - 1

    def build_bwd(step, bwd):
        right, _, keep, _ = shifts(step)
        init = tuple(pltpu.roll(base_b[ri, 0], right[g], 1) for ri, g in pairs)

        def one(n, carry):
            out = []
            for (ri, g), before in zip(pairs, carry):
                now = pltpu.roll(base_b[ri, n + 1], right[g], 1)
                bwd[ri, n + 1, rows(g)] = jnp.where(keep[g], now, before)
                out.append(now)
            return tuple(out)

        return init, one, ext - 1

    def add_shifted(total, shift, pick):
        def run(step, parts):
            amount, keep = shift(step)
            init = (zero8,) * 4

            def one(n, carry):
                out = []
                sums = [total[ri, n] for ri in range(2)]
                for (ri, g), before in zip(pairs, carry):
                    now = pltpu.roll(parts[ri, n, rows(g)], amount[g], 1)
                    sums[ri] = sums[ri] + pick(keep[g], now, before)
                    out.append(now)
                for ri in range(2):
                    total[ri, n] = sums[ri]
                return tuple(out)

            return init, one, ext

        return run

    def right_of(step):
        right, _, keep, _ = shifts(step)
        return right, keep

    def left_of(step):
        _, left, _, keep = shifts(step)
        return left, keep

    shear_up = add_shifted(up_all, right_of, lambda k, now, before: jnp.where(k, now, before))
    shear_lo = add_shifted(lo_all, left_of, lambda k, now, before: jnp.where(k, before, now))

    def run_all(task):
        init, one, count = task
        for n in range(count):
            init = one(n, init)

    @pl.when(pair == 0)
    def _():
        halo_part(
            nb, na, n_chan, n_sub, filter_ref, profile_ref, f_ref, q_ref,
            halo_low, halo_high, s_halo, r_halo,
        )
        for ri in range(2):
            high = jnp.broadcast_to(f_ref[ri, na:, :][:, None, :], (ext, 8, LANES))
            base_f[ri] = by_sublane(high, shift_left)
            low = jnp.broadcast_to(f_ref[ri, :ext, :][:, None, :], (ext, 8, LANES))
            base_b[ri] = by_sublane(low, shift_right)
        up_all[...] = jnp.zeros_like(up_all)
        lo_all[...] = jnp.zeros_like(lo_all)
        for _, _, up, lo in sets:
            up[...] = jnp.zeros_like(up)
            lo[...] = jnp.zeros_like(lo)
        err_acc[...] = jnp.zeros_like(err_acc)
        run_all(build_fwd(0 * pair, fwd0))
        run_all(build_bwd(0 * pair, bwd0))

    for half in range(2):
        m = 2 * pair + half
        held = slice(16 * half, 16 * half + 16)
        held_q = pl.ds(pl.multiple_of(16 * m, 16), 16)
        fwd, bwd, up, lo = sets[half]
        next_fwd, next_bwd, prev_up, prev_lo = sets[1 - half]
        for ri in range(2):
            for n in range(na - 1):
                up[ri, nb + n] = jnp.zeros((16, LANES), F32)
                lo[ri, n] = jnp.zeros((16, LANES), F32)

        tasks = [
            build_fwd(m + 1, next_fwd), build_bwd(m + 1, next_bwd),
            shear_up(m + last, prev_up), shear_lo(m + last, prev_lo),
        ]
        for a in range(na):
            qr = q_ref[0, a, held_q]
            qi = q_ref[1, a, held_q]
            init, side, count = tasks[a] if a < 4 else ((), lambda n, carry: carry, 0)

            def body(b, carry, a=a, qr=qr, qi=qi, side=side):
                gr, gi, er, beside = carry
                cols = pl.ds(pl.multiple_of(b * LANES, LANES), LANES)
                xr = x_ref[0, a, held, cols].astype(F32)
                xi = x_ref[1, a, held, cols].astype(F32)
                fr, fi = fwd[0, b + a], fwd[1, b + a]
                br, bi = bwd[0, b - a + na], bwd[1, b - a + na]
                beside = side(b, beside)
                pr = fr * br + fi * bi
                pi = fi * br - fr * bi
                rr = xr - (pr * qr - pi * qi)
                ri = xi - (pr * qi + pi * qr)
                er = er + (rr * rr + ri * ri)
                gr = gr + (rr * pr + ri * pi)
                gi = gi + (ri * pr - rr * pi)
                yr = rr * qr + ri * qi
                yi = ri * qr - rr * qi
                ur = yr * br - yi * bi
                ui = yr * bi + yi * br
                vr = yr * fr + yi * fi
                vi = yr * fi - yi * fr
                iu, il = b + a, b - a + na - 1
                if a == 0:
                    up[0, iu] = ur
                    up[1, iu] = ui
                    lo[0, il] = vr
                    lo[1, il] = vi
                else:
                    up[0, iu] = up[0, iu] + ur
                    up[1, iu] = up[1, iu] + ui
                    lo[0, il] = lo[0, il] + vr
                    lo[1, il] = lo[1, il] + vi
                return gr, gi, er, beside

            zero = jnp.zeros((16, LANES), F32)
            gr, gi, er, beside = lax.fori_loop(0, nb, body, (zero, zero, zero, init), unroll=nb)
            for n in range(nb, count):
                beside = side(n, beside)
            group = pl.ds(pl.multiple_of(16 * m, 16), 16)
            prof_acc[0, a, group] = gr
            prof_acc[1, a, group] = gi
            err_acc[...] = err_acc[...] + er
        for task in tasks[na:]:
            run_all(task)

    @pl.when(pair == last_pair)
    def _():
        run_all(shear_up(2 * pair + 1, up1))
        run_all(shear_lo(2 * pair + 1, lo1))
        for ri in range(2):
            upper = factor * jnp.sum(by_sublane(up_all[ri], shift_right), axis=1)
            lower = factor * jnp.sum(by_sublane(lo_all[ri], shift_left), axis=1)
            main_ref[ri * nb : (ri + 1) * nb] = upper[:nb] + lower[na:]
            tail_ref[ri * na : (ri + 1) * na] = upper[nb:]
            head_ref[ri * na : (ri + 1) * na] = lower[:na]
            for a in range(na):
                sums = lax.dot_general(
                    jnp.ones(tile, F32), prof_acc[ri, a], (((1,), (1,)), ((), ())),
                    precision=lax.Precision.HIGHEST, preferred_element_type=F32,
                )
                row = 2 * nb + ri * na + a
                main_ref[row : row + 1] = factor * sums[:1]
        main_ref[2 * nb + 2 * na :] = jnp.broadcast_to(
            jnp.sum(err_acc[...], axis=0, keepdims=True), tile
        )
        reduce_part(
            nb, na, n_chan, n_sub, harmonics, weight, main_ref, tail_ref, head_ref,
            out_ref, prof_ref, misfit_ref, *reduce_refs,
        )


def reduce_part(
    nb, na, n_chan, n_sub, harmonics, weight, main_ref, tail_ref, head_ref,
    out_ref, prof_ref, misfit_ref,
    mains, tails, heads, packs, pack,
    s_main, r_main, s_tail, r_tail, s_head, r_head, s_pack, r_pack,
):
    chan = lax.axis_index("chan")
    sub = lax.axis_index("sub")
    above = lax.rem(chan + 1, n_chan)
    below = lax.rem(chan + n_chan - 1, n_chan)

    def copy_to(src, dst, send, recv, device):
        return pltpu.make_async_remote_copy(
            src_ref=src, dst_ref=dst, send_sem=send, recv_sem=recv,
            device_id=device, device_id_type=MESH,
        )

    sends = []
    for off in range(1, n_sub):
        peer = lax.rem(sub + off, n_sub)
        sends.append(
            copy_to(main_ref, mains.at[sub], s_main.at[off], r_main.at[sub], (chan, peer))
        )
    for off in range(n_sub):
        peer = lax.rem(sub + off, n_sub)
        sends.append(
            copy_to(tail_ref, tails.at[sub], s_tail.at[off], r_tail.at[sub], (above, peer))
        )
        sends.append(
            copy_to(head_ref, heads.at[sub], s_head.at[off], r_head.at[sub], (below, peer))
        )
    for copy in sends:
        copy.start()
    mains[sub] = main_ref[...]
    for off in range(n_sub):
        peer = lax.rem(sub + off, n_sub)
        if off:
            copy_to(
                main_ref, mains.at[peer], s_main.at[off], r_main.at[peer], (chan, peer)
            ).wait_recv()
        copy_to(
            tail_ref, tails.at[peer], s_tail.at[off], r_tail.at[peer], (above, peer)
        ).wait_recv()
        copy_to(
            head_ref, heads.at[peer], s_head.at[off], r_head.at[peer], (below, peer)
        ).wait_recv()

    total = mains[0]
    tail = tails[0]
    head = heads[0]
    for s in range(1, n_sub):
        total = total + mains[s]
        tail = tail + tails[s]
        head = head + heads[s]
    tail = jnp.where(chan > 0, tail, 0.0)
    head = jnp.where(chan < n_chan - 1, head, 0.0)
    grads = []
    squares = jnp.zeros((1, LANES), F32)
    for ri in range(2):
        own = total[ri * nb : (ri + 1) * nb]
        part = slice(ri * na, (ri + 1) * na)
        grad = jnp.concatenate([own[:na] + tail[part], own[na:]], axis=0)
        grad = jnp.concatenate([grad[: nb - na], grad[nb - na :] + head[part]], axis=0)
        squares = squares + jnp.sum(grad * grad, axis=0, keepdims=True)
        grads.append(grad)
    prof_rows = 2 * na
    pack[...] = jnp.zeros_like(pack)
    pack[: prof_rows + 1] = total[2 * nb : 2 * nb + prof_rows + 1]
    pack[prof_rows + 1 : prof_rows + 2] = squares
    packs[chan] = pack[...]

    for copy in sends:
        copy.wait_send()
    exchanges = []
    for off in range(1, n_chan):
        peer = lax.rem(chan + off, n_chan)
        exchanges.append(
            copy_to(pack, packs.at[chan], s_pack.at[off], r_pack.at[chan], (peer, sub))
        )
    for copy in exchanges:
        copy.start()
    for off in range(1, n_chan):
        peer = lax.rem(chan + off, n_chan)
        copy_to(pack, packs.at[peer], s_pack.at[off], r_pack.at[peer], (peer, sub)).wait_recv()
    sums = packs[0]
    for c in range(1, n_chan):
        sums = sums + packs[c]
    prof_grad = sums[:prof_rows]
    error = jnp.sum(sums[prof_rows : prof_rows + 1])
    square = jnp.sum(sums[prof_rows + 1 : prof_rows + 2], axis=1, keepdims=True)
    channels = n_chan * nb * LANES
    misfit_ref[0] = error * (weight / channels)
    scale = filter_rate / jnp.sqrt(square / (2 * channels) + epsilon)
    for ri in range(2):
        step = grads[ri] * scale
        for n in range(nb):
            cols = slice(n * LANES, (n + 1) * LANES)
            out_ref[ri : ri + 1, cols] = step[n : n + 1]
    mean = jnp.sum(prof_grad * prof_grad, keepdims=True) / (2 * harmonics)
    prof_step = prof_grad * (profile_rate / jnp.sqrt(mean + epsilon))
    for ri in range(2):
        for a in range(na):
            cols = slice(a * LANES, (a + 1) * LANES)
            row = ri * na + a
            prof_ref[ri : ri + 1, cols] = prof_step[row : row + 1]
    for copy in exchanges:
        copy.wait_send()


def on_device(spectra, filter_init, profile_init):
    harmonics = profile_init.shape[1]
    owned = filter_init.shape[1]
    n_chan = lax.axis_size("chan")
    n_sub = lax.axis_size("sub")
    nb = owned // LANES
    na = harmonics // LANES
    ext = nb + na
    weight = 1.0 / (n_sub * spectra.shape[0] * harmonics)
    factor = -2.0 * weight
    main_rows = 2 * nb + 2 * na + 8

    whole = pl.BlockSpec(memory_space=pltpu.VMEM)
    dma = pltpu.SemaphoreType.DMA
    x = spectra.reshape(2, na, LANES, owned)

    strip = pltpu.VMEM((2, ext, 16, LANES), F32)
    base = pltpu.VMEM((2, ext, 8, LANES), F32)
    halo = pltpu.VMEM((2, harmonics), F32)
    scratch = [
        pltpu.VMEM((2, nb + 2 * na, LANES), F32),
        pltpu.VMEM((2, na, LANES, LANES), F32),
        halo, halo, dma((2,)), dma((2,)),
        pltpu.VMEM((main_rows, LANES), F32),
        pltpu.VMEM((2 * na, LANES), F32),
        pltpu.VMEM((2 * na, LANES), F32),
        [
            pltpu.VMEM((n_sub, main_rows, LANES), F32),
            pltpu.VMEM((n_sub, 2 * na, LANES), F32),
            pltpu.VMEM((n_sub, 2 * na, LANES), F32),
            pltpu.VMEM((n_chan, 2 * na + 8, LANES), F32),
            pltpu.VMEM((2 * na + 8, LANES), F32),
            dma((n_sub,)), dma((n_sub,)),
            dma((n_sub,)), dma((n_sub,)),
            dma((n_sub,)), dma((n_sub,)),
            dma((n_chan,)), dma((n_chan,)),
        ],
        base, base, *([strip] * 8), base, base,
        pltpu.VMEM((2, na, LANES, LANES), F32),
        pltpu.VMEM((16, LANES), F32),
    ]
    step, prof_step, misfit = pl.pallas_call(
        functools.partial(
            gradient_kernel, nb, na, n_chan, n_sub, harmonics, weight, factor
        ),
        grid=(LANES // 32,),
        in_specs=[
            whole, whole, pl.BlockSpec((2, na, 32, owned), lambda m: (0, 0, m, 0)),
        ],
        out_specs=[whole, whole, pl.BlockSpec(memory_space=pltpu.SMEM)],
        out_shape=[
            jax.ShapeDtypeStruct((2, owned), F32),
            jax.ShapeDtypeStruct((2, harmonics), F32),
            jax.ShapeDtypeStruct((1,), F32),
        ],
        scratch_shapes=scratch,
        compiler_params=pltpu.CompilerParams(collective_id=0, has_side_effects=True),
    )(filter_init, profile_init, x)
    return (filter_init - step, profile_init - prof_step, misfit)


def solution(mesh):
    return jax.shard_map(
        on_device,
        mesh=mesh,
        in_specs=(P("sub", None, None, "chan"), P(None, "chan"), P()),
        out_specs=(P(None, "chan"), P(), P()),
        check_vma=False,
    )
```
